256 devices in a mesh: lat: 16 (over y_lo, x, core), lon: 16 (over y_hi, z).
Axes of the slice: x: 4, y: 4 (y_hi: 2, y_lo: 2; y = y_hi * 2 + y_lo), z: 8, core: 2. Of those that a mesh axis runs over, the one named last changes fastest.
Arguments:
- fields: bfloat16 [32, 128, 4096], P(None, 'lat', 'lon'), may hold values from -6 to 6
- cotangent: bfloat16 [32, 128, 4096], P(None, 'lat', 'lon'), may hold values from -0.008239746 to 0.008239746
- kernel_in: bfloat16 [9, 128, 32], replicated, may hold values from -0.375 to 0.375
- kernel_mid: bfloat16 [9, 128, 128], replicated, may hold values from -0.1875 to 0.1875
- kernel_out: bfloat16 [9, 32, 128], replicated, may hold values from -0.1875 to 0.1875
- patch_anchors: int32 [16, 16, 4, 2], P('lat', 'lon'), may hold values from 0 to 8
- blend_weights: int32 [4, 128, 4096], P(None, 'lat', 'lon'), may hold values from 1 to 8
- tile_counts: int32 [16, 16], P('lat', 'lon'), may hold values from 0 to 4, as said below
Outputs:
- blended: float32 [32, 128, 4096], P(None, 'lat', 'lon')
- grad_in: float32 [9, 128, 32], replicated
- grad_mid: float32 [9, 128, 128], replicated
- grad_out: float32 [9, 32, 128], replicated
The draws below stay inside these ranges and needn't reach their ends.
Inputs may be any that keep to these rules, and one draw needn't show every extreme that they name: `tile_counts`: the counts of the tiles in lat rows i and i + 8 at the same lon sum to exactly 4; tile (1, 0) holds 4 patches and tile (9, 0) none.
All inputs are finite; a program needn't handle non-finite values.
Results may differ from the reference program's by a relative error of at most 0.005.
Values may be sent and summed in bfloat16 or wider, within the bound.
A program may use at most 64 MiB of HBM per device.

```python
import jax
import jax.numpy as jnp
from jax import lax

CHANNELS = 32
WIDTH = 128
TILE_ROWS = 8
TILE_COLS = 256
MARGIN = 4
SLOTS = 4
LAT_TILES = 16
LON_TILES = 16
ROWS = 128
COLS = 4096


def draw_tile_counts(key, part):
    first_half = jax.random.randint(key, (LAT_TILES // 2, LON_TILES), 1, SLOTS)
    first_half = first_half.at[1, 0].set(SLOTS)
    return jnp.concatenate([first_half, SLOTS - first_half], axis=0).astype(jnp.int32)


def with_ends(entries, stream_key, smallest, largest):
    longest = entries.shape.index(max(entries.shape))
    spots = []
    for shift in (0, 1):
        where = [jax.random.randint(jax.random.fold_in(stream_key, axis), (), 0, length) for axis, length in enumerate(entries.shape)]
        where[longest] = (where[longest] + shift) % entries.shape[longest]
        spots.append(tuple(where))
    return entries.at[spots[0]].set(smallest).at[spots[1]].set(largest)


def block_scale(stream_key, dims, shards, smallest, high):
    def one(axis_at, blocks):
        draws = jax.random.uniform(jax.random.fold_in(jax.random.fold_in(stream_key, 6), axis_at), (blocks,), jnp.float32, smallest / len(shards), high / len(shards))
        return jnp.repeat(jnp.exp(draws), dims[axis_at] // blocks).reshape((-1,) + (1,) * (len(dims) - axis_at - 1))

    gain = one(*shards[0])
    for cut in shards[1:]:
        gain = gain * one(*cut)
    return gain


def normal_values(key, shape, scale, most, shards=(), held_as=jnp.bfloat16):
    entries = jax.random.normal(key, shape, jnp.float32) * scale
    if len(shards) > 0:
        entries = block_scale(key, shape, shards, -0.22, 0.18) * entries
    return jnp.clip(entries, min=-most, max=most).astype(held_as)


def setup_inputs(seed: int = 0) -> dict:
    splits = jax.random.split(jax.random.key(seed), 9)
    fields = normal_values(splits[0], (CHANNELS, ROWS, COLS), 1.0, 6.0, ((1, 16), (2, 16)))
    cotangent = normal_values(splits[1], (CHANNELS, ROWS, COLS), ((ROWS * COLS) ** -0.5), 0.008239746, ((1, 16), (2, 16)))
    kernel_in = normal_values(splits[2], (9, WIDTH, CHANNELS), (9 * CHANNELS) ** -0.5, 0.375)
    kernel_mid = normal_values(splits[3], (9, WIDTH, WIDTH), (9 * WIDTH) ** -0.5, 0.1875)
    kernel_out = normal_values(splits[4], (9, CHANNELS, WIDTH), (9 * WIDTH) ** -0.5, 0.1875)
    patch_anchors = with_ends(jax.random.randint(splits[5], (LAT_TILES, LON_TILES, SLOTS, 2), 0, 2 * MARGIN + 1), jax.random.fold_in(splits[5], 1), 0, 2 * MARGIN).astype(jnp.int32)
    blend_weights = with_ends(jax.random.randint(splits[6], (SLOTS, ROWS, COLS), 1, 9), jax.random.fold_in(splits[6], 1), 1, 8).astype(jnp.int32)
    tile_counts = draw_tile_counts(jax.random.fold_in(splits[8], 71), 0)
    return {"fields": fields, "cotangent": cotangent, "kernel_in": kernel_in, "kernel_mid": kernel_mid, "kernel_out": kernel_out, "patch_anchors": patch_anchors, "blend_weights": blend_weights, "tile_counts": tile_counts}


KERNEL_TAPS = ((0, 0), (0, 1), (0, 2), (1, 0), (1, 1), (1, 2), (2, 0), (2, 1), (2, 2))

def contract(form, left_side, right_side):
    return jnp.einsum(form, left_side.astype(jnp.float32), right_side.astype(jnp.float32), precision=lax.Precision.HIGHEST)

def forward_conv(values, kernel):
    height, breadth = (values.shape[1], values.shape[2])
    padded = jnp.pad(values, ((0, 0), (1, 1), (1, 1)))
    summed = jnp.zeros((kernel.shape[1], height, breadth), jnp.float32)
    for tap_index, (tap_row, tap_col) in enumerate(KERNEL_TAPS):
        summed = summed + contract('ok,khw->ohw', kernel[tap_index], padded[:, tap_row:tap_row + height, tap_col:tap_col + breadth])
    return summed

def backward_conv(cotangent, kernel):
    height, breadth = (cotangent.shape[1], cotangent.shape[2])
    padded = jnp.pad(cotangent, ((0, 0), (1, 1), (1, 1)))
    summed = jnp.zeros((kernel.shape[2], height, breadth), jnp.float32)
    for tap_index, (tap_row, tap_col) in enumerate(KERNEL_TAPS):
        summed = summed + contract('ok,ohw->khw', kernel[tap_index], padded[:, 2 - tap_row:2 - tap_row + height, 2 - tap_col:2 - tap_col + breadth])
    return summed

def kernel_grad(cotangent, values):
    height, breadth = (values.shape[1], values.shape[2])
    padded = jnp.pad(values, ((0, 0), (1, 1), (1, 1)))
    pieces = [contract('ohw,khw->ok', cotangent, padded[:, tap_row:tap_row + height, tap_col:tap_col + breadth]) for tap_row, tap_col in KERNEL_TAPS]
    return jnp.stack(pieces)

def silu_slope(pre_act):
    sigmoid = jax.nn.sigmoid(pre_act)
    return sigmoid * (1.0 + pre_act * (1.0 - sigmoid))

def patch_pass(inputs, out_grad, kernel_in, kernel_mid, kernel_out):
    pre_one = forward_conv(inputs, kernel_in)
    hidden_one = jax.nn.silu(pre_one).astype(jnp.bfloat16)
    pre_two = forward_conv(hidden_one, kernel_mid)
    hidden_two = (hidden_one.astype(jnp.float32) + jax.nn.silu(pre_two)).astype(jnp.bfloat16)
    result = forward_conv(hidden_two, kernel_out)
    grad_two = backward_conv(out_grad, kernel_out)
    delta_two = (grad_two * silu_slope(pre_two)).astype(jnp.bfloat16)
    grad_one = grad_two + backward_conv(delta_two, kernel_mid)
    delta_one = (grad_one * silu_slope(pre_one)).astype(jnp.bfloat16)
    return (result, kernel_grad(delta_one, inputs), kernel_grad(delta_two, hidden_one), kernel_grad(out_grad, hidden_two))

def extend_field(values):
    wrapped = jnp.concatenate([values[:, :, COLS - MARGIN:], values, values[:, :, :MARGIN]], axis=2)
    return jnp.pad(wrapped, ((0, 0), (MARGIN, MARGIN), (0, 0)))

def fold_field(extended):
    center_part = extended[:, MARGIN:MARGIN + ROWS, MARGIN:MARGIN + COLS]
    left_rim = extended[:, MARGIN:MARGIN + ROWS, :MARGIN]
    right_rim = extended[:, MARGIN:MARGIN + ROWS, MARGIN + COLS:]
    center_part = center_part.at[:, :, :MARGIN].add(right_rim)
    center_part = center_part.at[:, :, COLS - MARGIN:].add(left_rim)
    return center_part

def reference(fields, cotangent, kernel_in, kernel_mid, kernel_out, patch_anchors, blend_weights, tile_counts):
    total_slots = LAT_TILES * LON_TILES * SLOTS
    slot_ids = jnp.arange(total_slots, dtype=jnp.int32)
    flat_counts = tile_counts.reshape(-1).astype(jnp.int32)
    alive_flags = (slot_ids % SLOTS < flat_counts[slot_ids // SLOTS]).astype(jnp.int32)
    live_order = jnp.argsort(1 - alive_flags, stable=True)[:total_slots // 2].astype(jnp.int32)

    def patch_info(flat_index):
        tile_id = flat_index // SLOTS
        slot_id = flat_index % SLOTS
        lat_id = tile_id // LON_TILES
        lon_id = tile_id % LON_TILES
        row_start = (lat_id * TILE_ROWS + patch_anchors[lat_id, lon_id, slot_id, 0]).astype(jnp.int32)
        col_start = (lon_id * TILE_COLS + patch_anchors[lat_id, lon_id, slot_id, 1]).astype(jnp.int32)
        weight = lax.dynamic_slice(blend_weights, (slot_id.astype(jnp.int32), (lat_id * TILE_ROWS).astype(jnp.int32), (lon_id * TILE_COLS).astype(jnp.int32)), (1, TILE_ROWS, TILE_COLS)).astype(jnp.float32)
        return (row_start, col_start, weight)

    def add_weight(canvas, flat_index):
        row_start, col_start, weight = patch_info(flat_index)
        corner = (jnp.int32(0), row_start, col_start)
        current = lax.dynamic_slice(canvas, corner, (1, TILE_ROWS, TILE_COLS))
        return (lax.dynamic_update_slice(canvas, current + weight, corner), None)
    weight_canvas = lax.scan(add_weight, jnp.zeros((1, ROWS + 2 * MARGIN, COLS + 2 * MARGIN), jnp.float32), live_order)[0]
    total_weight = jnp.maximum(fold_field(weight_canvas), 1.0)
    scaled = (cotangent.astype(jnp.float32) / total_weight).astype(jnp.bfloat16)
    wide_fields = extend_field(fields)
    wide_scaled = extend_field(scaled)

    def add_patch(running, flat_index):
        row_start, col_start, weight = patch_info(flat_index)
        corner = (jnp.int32(0), row_start, col_start)
        inputs = lax.dynamic_slice(wide_fields, corner, (CHANNELS, TILE_ROWS, TILE_COLS))
        out_grad = (weight * lax.dynamic_slice(wide_scaled, corner, (CHANNELS, TILE_ROWS, TILE_COLS)).astype(jnp.float32)).astype(jnp.bfloat16)
        result, part_in, part_mid, part_out = patch_pass(inputs, out_grad, kernel_in, kernel_mid, kernel_out)
        current = lax.dynamic_slice(running[0], corner, (CHANNELS, TILE_ROWS, TILE_COLS))
        numerator = lax.dynamic_update_slice(running[0], current + weight * result, corner)
        return ((numerator, running[1] + part_in, running[2] + part_mid, running[3] + part_out), None)
    initial = (jnp.zeros((CHANNELS, ROWS + 2 * MARGIN, COLS + 2 * MARGIN), jnp.float32), jnp.zeros(kernel_in.shape, jnp.float32), jnp.zeros(kernel_mid.shape, jnp.float32), jnp.zeros(kernel_out.shape, jnp.float32))
    finals = lax.scan(add_patch, initial, live_order)[0]
    blended = fold_field(finals[0]) / total_weight
    return (blended, finals[1], finals[2], finals[3])
```

```python
import functools

import jax
import jax.numpy as jnp
from jax import lax
from jax.experimental import pallas as pl
from jax.experimental.pallas import tpu as pltpu
from jax.sharding import PartitionSpec as P

MESH = pl.DeviceIdType.MESH
F32 = jnp.float32
BF16 = jnp.bfloat16

CH = 32
WD = 128
TR = 8
TC = 256
MG = 4
SLOTS = 4
EXT = 384
CELLS = TR * TC
PAD = (TR + 2) * TC

NB = ((-1, 0), (1, 0), (0, -1), (0, 1), (-1, -1), (-1, 1), (1, -1), (1, 1))
UP, DN, LF, RT, UL, UR, DL, DR = range(8)

G_MID, G_OUT, G_IN, G_END = 0, 9 * WD, 9 * WD + 9 * CH, 9 * WD + 18 * CH


def vmem(n):
    return [pl.BlockSpec(memory_space=pltpu.VMEM)] * n


def smem(n):
    return [pl.BlockSpec(memory_space=pltpu.SMEM)] * n


def lanes_of(shape):
    return lax.broadcasted_iota(jnp.int32, shape, len(shape) - 1)


def prep_kernel(anch, cnt, f_ref, c_ref, w_ref, fc_ref, e_ref, cv_ref, scr):
    for half in range(2):
        at = slice(half * 128, half * 128 + 128)
        scr[half] = f_ref[:, :, at].astype(F32).reshape(CH * TR, 128)
        scr[2 + half] = c_ref[:, :, at].astype(F32).reshape(CH * TR, 128)
    lane = lanes_of((2 * CH, 128))
    edge = jnp.zeros((2 * CH, 128), F32)
    for r in range(TR):
        piece = [scr[k, pl.ds(r, CH, stride=TR), :] for k in range(4)]
        row = jnp.concatenate(
            [jnp.concatenate(piece[:2], axis=1), jnp.concatenate(piece[2:], axis=1)], axis=0
        )
        fc_ref[r] = row.astype(BF16)
        first = pltpu.roll(row[:, :128], MG * r, 1) if r else row[:, :128]
        edge = jnp.where((lane >= MG * r) & (lane < MG * (r + 1)), first, edge)
        at = 32 + MG * r
        last = pltpu.roll(row[:, 128:], (at - (128 - MG)) % 128, 1)
        edge = jnp.where((lane >= at) & (lane < at + MG), last, edge)
    e_ref[...] = edge.astype(BF16)
    total = jnp.zeros((2 * TR, EXT), F32)
    for q in range(SLOTS):
        live = jnp.where(q < cnt[0, 0], 1.0, 0.0).astype(F32)
        w = w_ref[q].astype(F32) * live
        w = jnp.concatenate([w, jnp.zeros((TR, 128), F32)], axis=1)
        w = pltpu.roll(w, lax.rem(anch[q, 1] + (EXT - MG), EXT), 1)
        w = jnp.concatenate([w, jnp.zeros((TR, EXT), F32)], axis=0)
        total = total + pltpu.roll(w, anch[q, 0], 0)
    cv_ref[...] = total.astype(BF16)


def exchange_kernel(sizes, fc_ref, e_ref, cv_ref, up_ref, dn_ref, en_ref, cn_ref, ssem, rsem):
    la, lo = lax.axis_index("lat"), lax.axis_index("lon")
    nla, nlo = sizes
    where = [(lax.rem(la + di + nla, nla), lax.rem(lo + dj + nlo, nlo)) for di, dj in NB]
    barrier = pltpu.get_barrier_semaphore()
    for dev in where:
        pl.semaphore_signal(barrier, inc=1, device_id=dev, device_id_type=MESH)
    pl.semaphore_wait(barrier, len(NB))
    copies = []

    def send(src, dst, dev, k):
        copy = pltpu.make_async_remote_copy(
            src_ref=src, dst_ref=dst, send_sem=ssem.at[k], recv_sem=rsem.at[k],
            device_id=dev, device_id_type=MESH,
        )
        copy.start()
        copies.append(copy)

    send(fc_ref.at[0:MG], dn_ref, where[UP], 0)
    send(fc_ref.at[MG:TR], up_ref, where[DN], 1)
    for k, (di, dj) in enumerate(NB):
        back = NB.index((-di, -dj))
        send(cv_ref, cn_ref.at[back], where[k], 2 + back)
        if dj:
            send(e_ref, en_ref.at[back - 2], where[k], 10 + back - 2)
    for copy in copies:
        copy.wait()


def shift_cols(x, step):
    lane = lanes_of(x.shape)
    if step < 0:
        return jnp.where(lane == 0, 0.0, pltpu.roll(x, 1, 1))
    return jnp.where(lane == x.shape[1] - 1, 0.0, pltpu.roll(x, x.shape[1] - 1, 1))


def put_shifted(buf, r, x, ch):
    at = pl.multiple_of((r + 1) * TC, TC)
    buf[0:ch, pl.ds(at, TC)] = shift_cols(x, -1).astype(BF16)
    buf[ch : 2 * ch, pl.ds(at, TC)] = x.astype(BF16)
    buf[2 * ch : 3 * ch, pl.ds(at, TC)] = shift_cols(x, 1).astype(BF16)


def stacked(buf, r):
    return jnp.concatenate(
        [buf[:, pl.ds(pl.multiple_of((r + dy) * TC, TC), TC)] for dy in range(3)], axis=0
    )


def dot(a, b):
    return jnp.dot(a, b, preferred_element_type=F32)


def dot_t(a, b):
    return lax.dot_general(a, b, (((1,), (1,)), ((), ())), preferred_element_type=F32)


def patch_kernel(
    anch, cnt, fc_ref, up_ref, dn_ref, en_ref, cv_ref, cn_ref, w_ref, win_ref, wmid_ref, wout_ref,
    woutt_ref, wmidt_ref, num_ref, top_ref, bot_ref, np_ref, g_ref, inv_ref,
    ext, inv, xpb, dpb, h1b, dzb, h1, h2, sl1, sl2, dh2, dz1, oq, canvas, gmid, gout, gin,
):
    la, nla = lax.axis_index("lat"), lax.axis_size("lat")
    keep_top = la > 0
    keep_bot = la < nla - 1

    lane = lanes_of((2 * TR, EXT))
    den = cv_ref[...].astype(F32)

    def rows_of(k, canv):
        di = NB[k][0]
        zero = jnp.zeros((TR, EXT), F32)
        if di < 0:
            part = jnp.where(keep_top, canv[TR:], zero)
            return jnp.concatenate([part, zero], axis=0)
        if di > 0:
            part = jnp.where(keep_bot, canv[:TR], zero)
            return jnp.concatenate([zero, part], axis=0)
        return canv

    for k, (di, dj) in enumerate(NB):
        canv = cn_ref[k].astype(F32)
        if dj > 0:
            canv = jnp.concatenate([canv[:, 128:], canv[:, :128]], axis=1)
            canv = jnp.where((lane >= TC - MG) & (lane < TC + MG), canv, 0.0)
        if dj < 0:
            canv = jnp.concatenate([canv[:, 256:], canv[:, :256]], axis=1)
            canv = jnp.where((lane >= EXT - MG) | (lane < MG), canv, 0.0)
        den = den + rows_of(k, canv)
    inv[...] = 1.0 / jnp.maximum(den, 1.0)
    inv_ref[...] = inv[MG : MG + TR, :TC]

    hl = lanes_of((2 * CH, 128))
    for t in range(2 * TR):
        if t < MG:
            center, left, right, r, keep = up_ref[t], UL, UR, t + MG, keep_top
        elif t < MG + TR:
            center, left, right, r, keep = fc_ref[t - MG], LF, RT, t - MG, None
        else:
            center, left, right, r, keep = dn_ref[t - MG - TR], DL, DR, t - MG - TR, keep_bot
        lp = pltpu.roll(en_ref[left - 2].astype(F32), (96 - MG - MG * r) % 128, 1)
        rp = en_ref[right - 2].astype(F32)
        rp = pltpu.roll(rp, 128 - MG * r, 1) if r else rp
        row = jnp.concatenate([center.astype(F32), jnp.where(hl < 64, rp, lp)], axis=1)
        if keep is not None:
            row = jnp.where(keep, row, 0.0)
        ext[t, 0:CH, :] = row[:CH].astype(BF16)
        ext[t, CH:, :] = (row[CH:] * inv[t : t + 1, :]).astype(BF16)

    for buf in (xpb, dpb, h1b, dzb):
        z = jnp.zeros((buf.shape[0], TC), BF16)
        buf[:, 0:TC] = z
        buf[:, PAD - TC : PAD] = z
    canvas[...] = jnp.zeros_like(canvas)
    gmid[...] = jnp.zeros_like(gmid)
    gout[...] = jnp.zeros_like(gout)
    gin[...] = jnp.zeros_like(gin)

    def one_patch(q, carry):
        a, b = anch[q, 0], anch[q, 1]
        turn = lax.rem(EXT + MG - b, EXT)

        def window(r, c):
            x = pltpu.roll(ext[a + r].astype(F32), turn, 1)[:, :TC]
            pw = w_ref[q, pl.ds(r, 1), :].astype(F32)
            put_shifted(xpb, r, x[:CH], CH)
            put_shifted(dpb, r, x[CH:] * pw, CH)
            return c

        lax.fori_loop(0, TR, window, 0)

        def first(r, c):
            at = pl.ds(pl.multiple_of(r * TC, TC), TC)
            z = dot(win_ref[...], stacked(xpb, r))
            s = 0.5 + 0.5 * jnp.tanh(0.5 * z)
            h = z * s
            h1[:, at] = h.astype(BF16)
            put_shifted(h1b, r, h, WD)
            sl1[:, at] = s * (1.0 + z * (1.0 - s))
            return c

        lax.fori_loop(0, TR, first, 0)

        oq[...] = jnp.zeros_like(oq)

        def second(r, c):
            at = pl.ds(pl.multiple_of(r * TC, TC), TC)
            z = dot(wmid_ref[...], stacked(h1b, r))
            s = 0.5 + 0.5 * jnp.tanh(0.5 * z)
            h = (h1[:, at].astype(F32) + z * s).astype(BF16)
            h2[:, at] = h
            slope = s * (1.0 + z * (1.0 - s))
            p = dot(wout_ref[...], h)
            for dy in range(3):
                oq[r + 2 - dy] += p[dy * 96 : (dy + 1) * 96]
            g = dot(woutt_ref[...], stacked(dpb, r))
            dh2[:, at] = g
            put_shifted(dzb, r, g * slope, WD)
            return c

        lax.fori_loop(0, TR, second, 0)

        place = lax.rem(b + (EXT - MG), EXT)

        def blend(r, c):
            v = oq[r + 1]
            o = shift_cols(v[0:CH], -1) + v[CH : 2 * CH] + shift_cols(v[2 * CH :], 1)
            o = o * w_ref[q, pl.ds(r, 1), :].astype(F32)
            o = jnp.concatenate([o, jnp.zeros((CH, 128), F32)], axis=1)
            canvas[a + r] += pltpu.roll(o, place, 1)
            return c

        lax.fori_loop(0, TR, blend, 0)

        def third(r, c):
            at = pl.ds(pl.multiple_of(r * TC, TC), TC)
            g = dh2[:, at] + dot(wmidt_ref[...], stacked(dzb, r))
            dz1[:, at] = (g * sl1[:, at]).astype(BF16)
            return c

        lax.fori_loop(0, TR, third, 0)

        hh = h2[...]
        for dy in range(3):
            gout[dy] += dot_t(dpb[:, (2 - dy) * TC : (2 - dy) * TC + CELLS], hh)
        d1 = dz1[...]
        for dy in range(3):
            gin[dy] += dot_t(xpb[:, dy * TC : dy * TC + CELLS], d1)
        d2 = dzb[WD : 2 * WD, TC : TC + CELLS]
        for dy in range(3):
            gmid[:, dy * 384 : (dy + 1) * 384] += dot_t(d2, h1b[:, dy * TC : dy * TC + CELLS])
        return carry

    lax.fori_loop(0, cnt[0, 0], one_patch, 0)

    for r in range(TR):
        num_ref[r] = canvas[MG + r, :, :TC]
    for r in range(MG):
        top_ref[r] = canvas[r, :, :TC].astype(BF16)
        bot_ref[r] = canvas[MG + TR + r, :, :TC].astype(BF16)
    pk_lane = lanes_of((CH, 128))
    pk = jnp.zeros((CH, 128), F32)
    for t in range(2 * TR):
        v = canvas[t, :, TC:]
        hi = pltpu.roll(v, MG * t, 1) if t else v
        pk = jnp.where((pk_lane >= MG * t) & (pk_lane < MG * (t + 1)), hi, pk)
        at = 64 + MG * t
        lo = pltpu.roll(v, (at - (128 - MG)) % 128, 1)
        pk = jnp.where((pk_lane >= at) & (pk_lane < at + MG), lo, pk)
    np_ref[...] = pk.astype(BF16)
    for tap in range(9):
        g_ref[G_MID + tap * WD : G_MID + (tap + 1) * WD] = gmid[:, tap * WD : (tap + 1) * WD].astype(BF16)
        dy, dx = divmod(tap, 3)
        s = 2 - dx
        g_ref[G_OUT + tap * CH : G_OUT + (tap + 1) * CH] = gout[dy, s * CH : (s + 1) * CH].astype(BF16)
        g_ref[G_IN + tap * CH : G_IN + (tap + 1) * CH] = gin[dy, dx * CH : (dx + 1) * CH].astype(BF16)
    if g_ref.shape[0] > G_END:
        g_ref[G_END:] = jnp.zeros((g_ref.shape[0] - G_END, WD), BF16)


def reduce_kernel(
    sizes, parts, top_ref, bot_ref, np_ref, g_ref, nu_ref, nd_ref, n6_ref, gs_ref,
    buf1, buf2, mid, own, fin, ssem, rsem, s1, r1, s2, r2, s3, r3, s4, r4,
):
    la, lo = lax.axis_index("lat"), lax.axis_index("lon")
    nla, nlo = sizes
    pp = own.shape[0]
    where = [(lax.rem(la + di + nla, nla), lax.rem(lo + dj + nlo, nlo)) for di, dj in NB]
    lat_at = lambda k: lax.rem(la + k, nla)
    lon_at = lambda k: lax.rem(lo + k, nlo)
    barrier = pltpu.get_barrier_semaphore()
    for dev in where:
        pl.semaphore_signal(barrier, inc=1, device_id=dev, device_id_type=MESH)
    for k in range(1, nla):
        pl.semaphore_signal(barrier, inc=1, device_id=(lat_at(k), lo), device_id_type=MESH)
    for k in range(1, nlo):
        pl.semaphore_signal(barrier, inc=1, device_id=(la, lon_at(k)), device_id_type=MESH)
    pl.semaphore_wait(barrier, len(NB) + nla - 1 + nlo - 1)

    def copy_to(src, dst, ss, rs, dev):
        return pltpu.make_async_remote_copy(
            src_ref=src, dst_ref=dst, send_sem=ss, recv_sem=rs, device_id=dev, device_id_type=MESH
        )

    first = []
    for k in range(1, nla):
        to = lat_at(k)
        first.append(copy_to(g_ref.at[to], buf1.at[nla - k], s1.at[k], r1.at[nla - k], (to, lo)))
    for c in first:
        c.start()
    edges = [
        copy_to(top_ref, nd_ref, ssem.at[0], rsem.at[0], where[UP]),
        copy_to(bot_ref, nu_ref, ssem.at[1], rsem.at[1], where[DN]),
    ]
    for k, (di, dj) in enumerate(NB):
        if dj:
            back = NB.index((-di, -dj)) - 2
            edges.append(copy_to(np_ref, n6_ref.at[back], ssem.at[2 + back], rsem.at[2 + back], where[k]))
    for c in edges:
        c.start()
    total = g_ref[la].astype(F32)
    for k in range(1, nla):
        copy_to(g_ref.at[la], buf1.at[k], s1.at[nla - k], r1.at[k], (la, lo)).wait_recv()
        total = total + buf1[k].astype(F32)
    mid[...] = total

    second = []
    for k in range(1, nlo):
        to = lon_at(k)
        c = copy_to(mid.at[pl.ds(jnp.minimum(to * pp, parts - pp), pp)], buf2.at[nlo - k], s2.at[k], r2.at[nlo - k], (la, to))
        c.start()
        second.append(c)
    piece = mid[pl.ds(jnp.minimum(lo * pp, parts - pp), pp)]
    for k in range(1, nlo):
        copy_to(mid.at[0:pp], buf2.at[k], s2.at[k], r2.at[k], (la, lo)).wait_recv()
        piece = piece + buf2[k]
    own[...] = piece.astype(BF16)

    third = []
    for k in range(1, nlo):
        c = copy_to(own, fin.at[pl.ds(lo * pp, pp)], s3.at[k], r3.at[nlo - k], (la, lon_at(k)))
        c.start()
        third.append(c)
    fin[pl.ds(lo * pp, pp)] = own[...]
    for k in range(1, nlo):
        copy_to(own, fin.at[pl.ds(lon_at(k) * pp, pp)], s3.at[k], r3.at[k], (la, lo)).wait_recv()

    fourth = []
    for k in range(1, nla):
        c = copy_to(fin.at[0:parts], gs_ref.at[la], s4.at[k], r4.at[nla - k], (lat_at(k), lo))
        c.start()
        fourth.append(c)
    gs_ref[la] = fin[0:parts]
    for k in range(1, nla):
        copy_to(fin.at[0:parts], gs_ref.at[lat_at(k)], s4.at[k], r4.at[k], (la, lo)).wait_recv()
    for c in edges:
        c.wait_recv()
    for c in edges + first + second + third + fourth:
        c.wait_send()


def finish_kernel(num_ref, inv_ref, nu_ref, nd_ref, n6_ref, g_ref, b_ref, gi_ref, gm_ref, go_ref, scr):
    la, nla = lax.axis_index("lat"), lax.axis_size("lat")
    keep_top = jnp.where(la > 0, 1.0, 0.0).astype(F32)
    keep_bot = jnp.where(la < nla - 1, 1.0, 0.0).astype(F32)
    lane = lanes_of((CH, 128))

    def left_of(k, t):
        v = pltpu.roll(n6_ref[k - 2].astype(F32), (128 - MG * t) % 128, 1) if t else n6_ref[k - 2].astype(F32)
        return jnp.where(lane < MG, v, 0.0)

    def right_of(k, t):
        v = pltpu.roll(n6_ref[k - 2].astype(F32), (64 - MG - MG * t) % 128, 1)
        return jnp.where(lane >= 128 - MG, v, 0.0)

    for r in range(TR):
        v = num_ref[r]
        if r < MG:
            v = v + keep_top * nu_ref[r].astype(F32)
            hl = left_of(LF, r + MG) + keep_top * left_of(UL, r + MG + TR)
            hr = right_of(RT, r + MG) + keep_top * right_of(UR, r + MG + TR)
        else:
            v = v + keep_bot * nd_ref[r - MG].astype(F32)
            hl = left_of(LF, r + MG) + keep_bot * left_of(DL, r - MG)
            hr = right_of(RT, r + MG) + keep_bot * right_of(DR, r - MG)
        v = v + jnp.concatenate([hl, hr], axis=1)
        v = v * inv_ref[r : r + 1, :]
        for half in range(2):
            scr[half, pl.ds(r, CH, stride=TR), :] = v[:, half * 128 : half * 128 + 128]
    for half in range(2):
        b_ref[:, half * 128 : half * 128 + 128] = scr[half]
    for tap in range(9):
        gm_ref[tap] = g_ref[G_MID + tap * WD : G_MID + (tap + 1) * WD].astype(F32)
        go_ref[tap] = g_ref[G_OUT + tap * CH : G_OUT + (tap + 1) * CH].astype(F32)
        gi_ref[tap] = g_ref[G_IN + tap * CH : G_IN + (tap + 1) * CH].astype(F32).T


def sds(shape, dtype):
    return jax.ShapeDtypeStruct(shape, dtype)


def shards(sizes, fields, cotangent, kernel_in, kernel_mid, kernel_out, patch_anchors, blend_weights, tile_counts):
    nla, nlo = sizes
    anch = patch_anchors[0, 0]
    dma = pltpu.SemaphoreType.DMA
    fc, edge, canv = pl.pallas_call(
        prep_kernel,
        name="prepare",
        out_shape=(sds((TR, 2 * CH, TC), BF16), sds((2 * CH, 128), BF16), sds((2 * TR, EXT), BF16)),
        in_specs=smem(2) + vmem(3),
        out_specs=vmem(3),
        scratch_shapes=[pltpu.VMEM((4, CH * TR, 128), F32)],
    )(anch, tile_counts, fields, cotangent, blend_weights)

    up, dn, en, cn = pl.pallas_call(
        functools.partial(exchange_kernel, sizes),
        name="exchange",
        out_shape=(
            sds((MG, 2 * CH, TC), BF16), sds((MG, 2 * CH, TC), BF16),
            sds((6, 2 * CH, 128), BF16), sds((8, 2 * TR, EXT), BF16),
        ),
        in_specs=vmem(3),
        out_specs=vmem(4),
        scratch_shapes=[dma((16,)), dma((16,))],
        compiler_params=pltpu.CompilerParams(collective_id=0, has_side_effects=True),
    )(fc, edge, canv)

    win = kernel_in.transpose(1, 0, 2).reshape(WD, 9 * CH)
    wmid = kernel_mid.transpose(1, 0, 2).reshape(WD, 9 * WD)
    wout = kernel_out.reshape(9 * CH, WD)
    woutt = kernel_out[::-1].transpose(2, 0, 1).reshape(WD, 9 * CH)
    wmidt = kernel_mid[::-1].transpose(2, 0, 1).reshape(WD, 9 * WD)

    parts = -(-(G_END // 8) // nla)
    pp = -(-parts // nlo)
    grow = nla * parts * 8
    vm = pltpu.VMEM
    num, top, bot, npk, grads, inv = pl.pallas_call(
        patch_kernel,
        name="patches",
        out_shape=(
            sds((TR, CH, TC), F32), sds((MG, CH, TC), BF16), sds((MG, CH, TC), BF16),
            sds((CH, 128), BF16), sds((grow, WD), BF16), sds((TR, TC), F32),
        ),
        in_specs=smem(2) + vmem(12),
        out_specs=vmem(6),
        scratch_shapes=[
            vm((2 * TR, 2 * CH, EXT), BF16), vm((2 * TR, EXT), F32),
            vm((3 * CH, PAD), BF16), vm((3 * CH, PAD), BF16), vm((3 * WD, PAD), BF16), vm((3 * WD, PAD), BF16),
            vm((WD, CELLS), BF16), vm((WD, CELLS), BF16), vm((WD, CELLS), F32), vm((8, 128), F32),
            vm((WD, CELLS), F32), vm((WD, CELLS), BF16), vm((TR + 2, 3 * CH, TC), F32),
            vm((2 * TR, CH, EXT), F32), vm((WD, 9 * WD), F32), vm((3, 3 * CH, WD), F32), vm((3, 3 * CH, WD), F32),
        ],
    )(anch, tile_counts, fc, up, dn, en, canv, cn, blend_weights, win, wmid, wout, woutt, wmidt)

    nu, nd, n6, gs = pl.pallas_call(
        functools.partial(reduce_kernel, sizes, parts),
        name="reduce",
        out_shape=(
            sds((MG, CH, TC), BF16), sds((MG, CH, TC), BF16), sds((6, CH, 128), BF16),
            sds((nla, parts, 8, WD), BF16),
        ),
        in_specs=vmem(4),
        out_specs=vmem(4),
        scratch_shapes=[
            vm((nla, parts, 8, WD), BF16), vm((nlo, pp, 8, WD), F32), vm((parts, 8, WD), F32),
            vm((pp, 8, WD), BF16), vm((nlo * pp, 8, WD), BF16),
            dma((8,)), dma((8,)), dma((nla,)), dma((nla,)), dma((nlo,)), dma((nlo,)),
            dma((nlo,)), dma((nlo,)), dma((nla,)), dma((nla,)),
        ],
        compiler_params=pltpu.CompilerParams(collective_id=1, has_side_effects=True),
    )(top, bot, npk, grads.reshape(nla, parts, 8, WD))

    blended, gi, gm, go = pl.pallas_call(
        finish_kernel,
        name="finish",
        out_shape=(
            sds((CH * TR, TC), F32), sds((9, WD, CH), F32), sds((9, WD, WD), F32), sds((9, CH, WD), F32),
        ),
        in_specs=vmem(6),
        out_specs=vmem(4),
        scratch_shapes=[vm((2, CH * TR, 128), F32)],
    )(num, inv, nu, nd, n6, gs.reshape(grow, WD))
    return blended.reshape(CH, TR, TC), gi, gm, go


def solution(mesh):
    sizes = (mesh.shape["lat"], mesh.shape["lon"])
    return jax.shard_map(
        functools.partial(shards, sizes),
        mesh=mesh,
        in_specs=(
            P(None, "lat", "lon"), P(None, "lat", "lon"), P(), P(), P(),
            P("lat", "lon", None, None), P(None, "lat", "lon"), P("lat", "lon"),
        ),
        out_specs=(P(None, "lat", "lon"), P(), P(), P()),
        check_vma=False,
    )
```

```python
import functools

import jax
import jax.numpy as jnp
from jax import lax
from jax.experimental import pallas as pl
from jax.experimental.pallas import tpu as pltpu
from jax.sharding import PartitionSpec as P

MESH = pl.DeviceIdType.MESH
F32 = jnp.float32
BF16 = jnp.bfloat16

CH = 32
WD = 128
TR = 8
TC = 256
MG = 4
SLOTS = 4
EXT = 384
CELLS = TR * TC
PAD = (TR + 2) * TC

NB = ((-1, 0), (1, 0), (0, -1), (0, 1), (-1, -1), (-1, 1), (1, -1), (1, 1))
UP, DN, LF, RT, UL, UR, DL, DR = range(8)

G_MID, G_OUT, G_IN, G_END = 0, 9 * WD, 9 * WD + 9 * CH, 9 * WD + 18 * CH


def vmem(n):
    return [pl.BlockSpec(memory_space=pltpu.VMEM)] * n


def smem(n):
    return [pl.BlockSpec(memory_space=pltpu.SMEM)] * n


def lanes_of(shape):
    return lax.broadcasted_iota(jnp.int32, shape, len(shape) - 1)


def prep_kernel(anch, cnt, f_ref, c_ref, w_ref, fc_ref, e_ref, cv_ref, scr):
    for half in range(2):
        at = slice(half * 128, half * 128 + 128)
        scr[half] = f_ref[:, :, at].astype(F32).reshape(CH * TR, 128)
        scr[2 + half] = c_ref[:, :, at].astype(F32).reshape(CH * TR, 128)
    lane = lanes_of((2 * CH, 128))
    edge = jnp.zeros((2 * CH, 128), F32)
    for r in range(TR):
        piece = [scr[k, pl.ds(r, CH, stride=TR), :] for k in range(4)]
        row = jnp.concatenate(
            [jnp.concatenate(piece[:2], axis=1), jnp.concatenate(piece[2:], axis=1)], axis=0
        )
        fc_ref[r] = row.astype(BF16)
        first = pltpu.roll(row[:, :128], MG * r, 1) if r else row[:, :128]
        edge = jnp.where((lane >= MG * r) & (lane < MG * (r + 1)), first, edge)
        at = 32 + MG * r
        last = pltpu.roll(row[:, 128:], (at - (128 - MG)) % 128, 1)
        edge = jnp.where((lane >= at) & (lane < at + MG), last, edge)
    e_ref[...] = edge.astype(BF16)
    total = jnp.zeros((2 * TR, EXT), F32)
    for q in range(SLOTS):
        live = jnp.where(q < cnt[0, 0], 1.0, 0.0).astype(F32)
        w = w_ref[q].astype(F32) * live
        w = jnp.concatenate([w, jnp.zeros((TR, 128), F32)], axis=1)
        w = pltpu.roll(w, lax.rem(anch[q, 1] + (EXT - MG), EXT), 1)
        w = jnp.concatenate([w, jnp.zeros((TR, EXT), F32)], axis=0)
        total = total + pltpu.roll(w, anch[q, 0], 0)
    cv_ref[...] = total.astype(BF16)


def exchange_kernel(sizes, fc_ref, e_ref, cv_ref, up_ref, dn_ref, en_ref, cn_ref, ssem, rsem):
    la, lo = lax.axis_index("lat"), lax.axis_index("lon")
    nla, nlo = sizes
    where = [(lax.rem(la + di + nla, nla), lax.rem(lo + dj + nlo, nlo)) for di, dj in NB]
    barrier = pltpu.get_barrier_semaphore()
    for dev in where:
        pl.semaphore_signal(barrier, inc=1, device_id=dev, device_id_type=MESH)
    pl.semaphore_wait(barrier, len(NB))
    copies = []

    def send(src, dst, dev, k):
        copy = pltpu.make_async_remote_copy(
            src_ref=src, dst_ref=dst, send_sem=ssem.at[k], recv_sem=rsem.at[k],
            device_id=dev, device_id_type=MESH,
        )
        copy.start()
        copies.append(copy)

    send(fc_ref.at[0:MG], dn_ref, where[UP], 0)
    send(fc_ref.at[MG:TR], up_ref, where[DN], 1)
    for k, (di, dj) in enumerate(NB):
        back = NB.index((-di, -dj))
        send(cv_ref, cn_ref.at[back], where[k], 2 + back)
        if dj:
            send(e_ref, en_ref.at[back - 2], where[k], 10 + back - 2)
    for copy in copies:
        copy.wait()


def shift_cols(x, step):
    lane = lanes_of((x.shape[0], 128))
    lo, hi = x[:, :128], x[:, 128:]
    zero = jnp.zeros_like(lo)
    if step < 0:
        lo, hi = pltpu.roll(lo, 1, 1), pltpu.roll(hi, 1, 1)
        return jnp.concatenate([jnp.where(lane == 0, zero, lo), jnp.where(lane == 0, lo, hi)], axis=1)
    lo, hi = pltpu.roll(lo, 127, 1), pltpu.roll(hi, 127, 1)
    return jnp.concatenate([jnp.where(lane == 127, hi, lo), jnp.where(lane == 127, zero, hi)], axis=1)


def put_shifted(buf, r, x, ch):
    at = slice((r + 1) * TC, (r + 2) * TC)
    buf[0:ch, at] = shift_cols(x, -1)
    buf[ch : 2 * ch, at] = x
    buf[2 * ch : 3 * ch, at] = shift_cols(x, 1)


def four_rows(buf, i, rows=slice(None)):
    return jnp.concatenate([buf[rows, (2 * i + j) * TC : (2 * i + j + 1) * TC] for j in range(4)], axis=0)


def dot(a, b):
    return jnp.dot(a, b, preferred_element_type=F32)


def dot_t(a, b):
    return lax.dot_general(a, b, (((1,), (1,)), ((), ())), preferred_element_type=F32)


def patch_kernel(
    anch, cnt, fc_ref, up_ref, dn_ref, en_ref, cv_ref, cn_ref, w_ref, win_ref, wmid_ref, wout_ref,
    woutt_ref, wmidt_ref, num_ref, top_ref, bot_ref, np_ref, g_ref, inv_ref,
    ext, inv, xpb, dpb, h1b, dzb, h2b, sl1, dh2, dz1, canvas, gmid, gout, gin,
):
    la, nla = lax.axis_index("lat"), lax.axis_size("lat")
    keep_top = la > 0
    keep_bot = la < nla - 1

    lane = lanes_of((2 * TR, EXT))
    den = cv_ref[...].astype(F32)

    def rows_of(k, canv):
        di = NB[k][0]
        zero = jnp.zeros((TR, EXT), F32)
        if di < 0:
            part = jnp.where(keep_top, canv[TR:], zero)
            return jnp.concatenate([part, zero], axis=0)
        if di > 0:
            part = jnp.where(keep_bot, canv[:TR], zero)
            return jnp.concatenate([zero, part], axis=0)
        return canv

    for k, (di, dj) in enumerate(NB):
        canv = cn_ref[k].astype(F32)
        if dj > 0:
            canv = jnp.concatenate([canv[:, 128:], canv[:, :128]], axis=1)
            canv = jnp.where((lane >= TC - MG) & (lane < TC + MG), canv, 0.0)
        if dj < 0:
            canv = jnp.concatenate([canv[:, 256:], canv[:, :256]], axis=1)
            canv = jnp.where((lane >= EXT - MG) | (lane < MG), canv, 0.0)
        den = den + rows_of(k, canv)
    inv[...] = 1.0 / jnp.maximum(den, 1.0)
    inv_ref[...] = inv[MG : MG + TR, :TC]

    hl = lanes_of((2 * CH, 128))
    for t in range(2 * TR):
        if t < MG:
            center, left, right, r, keep = up_ref[t], UL, UR, t + MG, keep_top
        elif t < MG + TR:
            center, left, right, r, keep = fc_ref[t - MG], LF, RT, t - MG, None
        else:
            center, left, right, r, keep = dn_ref[t - MG - TR], DL, DR, t - MG - TR, keep_bot
        lp = pltpu.roll(en_ref[left - 2].astype(F32), (96 - MG - MG * r) % 128, 1)
        rp = en_ref[right - 2].astype(F32)
        rp = pltpu.roll(rp, 128 - MG * r, 1) if r else rp
        row = jnp.concatenate([center.astype(F32), jnp.where(hl < 64, rp, lp)], axis=1)
        if keep is not None:
            row = jnp.where(keep, row, 0.0)
        ext[t, 0:CH, :] = row[:CH].astype(BF16)
        ext[t, CH:, :] = (row[CH:] * inv[t : t + 1, :]).astype(BF16)

    for buf in (xpb, dpb, h1b, dzb, h2b):
        z = jnp.zeros((buf.shape[0], TC), BF16)
        buf[:, 0:TC] = z
        buf[:, PAD - TC : PAD] = z
    canvas[...] = jnp.zeros_like(canvas)
    gmid[...] = jnp.zeros_like(gmid)
    gout[...] = jnp.zeros_like(gout)
    gin[...] = jnp.zeros_like(gin)

    def one_patch(q, carry):
        a, b = anch[q, 0], anch[q, 1]
        turn = lax.rem(EXT + MG - b, EXT)
        place = lax.rem(b + (EXT - MG), EXT)
        weights = w_ref[q].astype(F32)

        def rows(i):
            return range(2 * i, 2 * i + 2)

        def at(r):
            return slice(r * TC, (r + 1) * TC)

        def half(z, r):
            n = z.shape[0] // 2
            return z[:n] if r % 2 == 0 else z[n:]

        def window(i):
            for r in rows(i):
                x = pltpu.roll(ext[a + r].astype(F32), turn, 1)[:, :TC]
                put_shifted(xpb, r, x[:CH].astype(BF16), CH)
                put_shifted(dpb, r, (x[CH:] * weights[r : r + 1, :]).astype(BF16), CH)

        def first(i):
            zz = dot(win_ref[...], four_rows(xpb, i))
            for r in rows(i):
                z = half(zz, r)
                t = jnp.tanh(0.5 * z)
                s = 0.5 + 0.5 * t
                h = z * s
                put_shifted(h1b, r, h.astype(BF16), WD)
                sl1[:, at(r)] = s + h * (1.0 - s)

        def second(i):
            zz = dot(wmid_ref[...], four_rows(h1b, i))
            gg = dot(woutt_ref[...], four_rows(dpb, i))
            for r in rows(i):
                z, g = half(zz, r), half(gg, r)
                t = jnp.tanh(0.5 * z)
                s = 0.5 + 0.5 * t
                h = z * s
                h2b[:, at(r + 1)] = (h1b[WD : 2 * WD, at(r + 1)].astype(F32) + h).astype(BF16)
                dh2[:, at(r)] = g
                put_shifted(dzb, r, (g * (s + h * (1.0 - s))).astype(BF16), WD)

        def blend(i):
            oo = dot(wout_ref[...], four_rows(h2b, i))
            for r in rows(i):
                v = half(oo, r)
                o = shift_cols(v[0:CH], -1) + v[CH : 2 * CH] + shift_cols(v[2 * CH :], 1)
                o = o * weights[r : r + 1, :]
                o = jnp.concatenate([o, jnp.zeros((CH, 128), F32)], axis=1)
                canvas[a + r] += pltpu.roll(o, place, 1)

        def third(i):
            zz = dot(wmidt_ref[...], four_rows(dzb, i))
            for r in rows(i):
                g = dh2[:, at(r)] + half(zz, r)
                dz1[:, at(r)] = (g * sl1[:, at(r)]).astype(BF16)

        window(0)
        window(1)
        first(0)
        window(2)
        first(1)
        window(3)
        second(0)
        first(2)
        second(1)
        first(3)
        third(0)
        blend(0)
        second(2)
        third(1)
        blend(1)
        second(3)
        third(2)
        blend(2)
        third(3)
        blend(3)

        hh = h2b[:, TC : TC + CELLS]
        d1 = dz1[...]
        d2 = dzb[0 : 2 * WD, TC : TC + CELLS]
        for dy in range(3):
            gmid[dy] += dot_t(d2, h1b[0 : 2 * WD, dy * TC : dy * TC + CELLS])
            gout[dy] += dot_t(dpb[:, (2 - dy) * TC : (2 - dy) * TC + CELLS], hh)
            gin[dy] += dot_t(xpb[:, dy * TC : dy * TC + CELLS], d1)
        return carry

    lax.fori_loop(0, cnt[0, 0], one_patch, 0)

    for r in range(TR):
        num_ref[r] = canvas[MG + r, :, :TC]
    for r in range(MG):
        top_ref[r] = canvas[r, :, :TC].astype(BF16)
        bot_ref[r] = canvas[MG + TR + r, :, :TC].astype(BF16)
    pk_lane = lanes_of((CH, 128))
    pk = jnp.zeros((CH, 128), F32)
    for t in range(2 * TR):
        v = canvas[t, :, TC:]
        hi = pltpu.roll(v, MG * t, 1) if t else v
        pk = jnp.where((pk_lane >= MG * t) & (pk_lane < MG * (t + 1)), hi, pk)
        at = 64 + MG * t
        lo = pltpu.roll(v, (at - (128 - MG)) % 128, 1)
        pk = jnp.where((pk_lane >= at) & (pk_lane < at + MG), lo, pk)
    np_ref[...] = pk.astype(BF16)
    for tap in range(9):
        dy, dx = divmod(tap, 3)
        ro, co = ((1, 0), (1, 1), (0, 1))[dx]
        g_ref[G_MID + tap * WD : G_MID + (tap + 1) * WD] = gmid[
            dy, ro * WD : (ro + 1) * WD, co * WD : (co + 1) * WD
        ].astype(BF16)
        s = 2 - dx
        g_ref[G_OUT + tap * CH : G_OUT + (tap + 1) * CH] = gout[dy, s * CH : (s + 1) * CH].astype(BF16)
        g_ref[G_IN + tap * CH : G_IN + (tap + 1) * CH] = gin[dy, dx * CH : (dx + 1) * CH].astype(BF16)
    if g_ref.shape[0] > G_END:
        g_ref[G_END:] = jnp.zeros((g_ref.shape[0] - G_END, WD), BF16)


def reduce_kernel(
    sizes, parts, top_ref, bot_ref, np_ref, g_ref, nu_ref, nd_ref, n6_ref, gs_ref,
    buf1, buf2, mid, own, fin, ssem, rsem, s1, r1, s2, r2, s3, r3, s4, r4,
):
    la, lo = lax.axis_index("lat"), lax.axis_index("lon")
    nla, nlo = sizes
    pp = own.shape[0]
    where = [(lax.rem(la + di + nla, nla), lax.rem(lo + dj + nlo, nlo)) for di, dj in NB]
    lat_at = lambda k: lax.rem(la + k, nla)
    lon_at = lambda k: lax.rem(lo + k, nlo)
    barrier = pltpu.get_barrier_semaphore()
    for dev in where:
        pl.semaphore_signal(barrier, inc=1, device_id=dev, device_id_type=MESH)
    for k in range(1, nla):
        pl.semaphore_signal(barrier, inc=1, device_id=(lat_at(k), lo), device_id_type=MESH)
    for k in range(1, nlo):
        pl.semaphore_signal(barrier, inc=1, device_id=(la, lon_at(k)), device_id_type=MESH)
    pl.semaphore_wait(barrier, len(NB) + nla - 1 + nlo - 1)

    def copy_to(src, dst, ss, rs, dev):
        return pltpu.make_async_remote_copy(
            src_ref=src, dst_ref=dst, send_sem=ss, recv_sem=rs, device_id=dev, device_id_type=MESH
        )

    first = []
    for k in range(1, nla):
        to = lat_at(k)
        first.append(copy_to(g_ref.at[to], buf1.at[nla - k], s1.at[k], r1.at[nla - k], (to, lo)))
    for c in first:
        c.start()
    edges = [
        copy_to(top_ref, nd_ref, ssem.at[0], rsem.at[0], where[UP]),
        copy_to(bot_ref, nu_ref, ssem.at[1], rsem.at[1], where[DN]),
    ]
    for k, (di, dj) in enumerate(NB):
        if dj:
            back = NB.index((-di, -dj)) - 2
            edges.append(copy_to(np_ref, n6_ref.at[back], ssem.at[2 + back], rsem.at[2 + back], where[k]))
    for c in edges:
        c.start()
    total = g_ref[la].astype(F32)
    for k in range(1, nla):
        copy_to(g_ref.at[la], buf1.at[k], s1.at[nla - k], r1.at[k], (la, lo)).wait_recv()
        total = total + buf1[k].astype(F32)
    mid[...] = total

    second = []
    for k in range(1, nlo):
        to = lon_at(k)
        c = copy_to(mid.at[pl.ds(jnp.minimum(to * pp, parts - pp), pp)], buf2.at[nlo - k], s2.at[k], r2.at[nlo - k], (la, to))
        c.start()
        second.append(c)
    piece = mid[pl.ds(jnp.minimum(lo * pp, parts - pp), pp)]
    for k in range(1, nlo):
        copy_to(mid.at[0:pp], buf2.at[k], s2.at[k], r2.at[k], (la, lo)).wait_recv()
        piece = piece + buf2[k]
    own[...] = piece.astype(BF16)

    third = []
    for k in range(1, nlo):
        c = copy_to(own, fin.at[pl.ds(lo * pp, pp)], s3.at[k], r3.at[nlo - k], (la, lon_at(k)))
        c.start()
        third.append(c)
    fin[pl.ds(lo * pp, pp)] = own[...]
    for k in range(1, nlo):
        copy_to(own, fin.at[pl.ds(lon_at(k) * pp, pp)], s3.at[k], r3.at[k], (la, lo)).wait_recv()

    fourth = []
    for k in range(1, nla):
        c = copy_to(fin.at[0:parts], gs_ref.at[la], s4.at[k], r4.at[nla - k], (lat_at(k), lo))
        c.start()
        fourth.append(c)
    gs_ref[la] = fin[0:parts]
    for k in range(1, nla):
        copy_to(fin.at[0:parts], gs_ref.at[lat_at(k)], s4.at[k], r4.at[k], (la, lo)).wait_recv()
    for c in edges:
        c.wait_recv()
    for c in edges + first + second + third + fourth:
        c.wait_send()


def finish_kernel(num_ref, inv_ref, nu_ref, nd_ref, n6_ref, g_ref, b_ref, gi_ref, gm_ref, go_ref, scr):
    la, nla = lax.axis_index("lat"), lax.axis_size("lat")
    keep_top = jnp.where(la > 0, 1.0, 0.0).astype(F32)
    keep_bot = jnp.where(la < nla - 1, 1.0, 0.0).astype(F32)
    lane = lanes_of((CH, 128))

    def left_of(k, t):
        v = pltpu.roll(n6_ref[k - 2].astype(F32), (128 - MG * t) % 128, 1) if t else n6_ref[k - 2].astype(F32)
        return jnp.where(lane < MG, v, 0.0)

    def right_of(k, t):
        v = pltpu.roll(n6_ref[k - 2].astype(F32), (64 - MG - MG * t) % 128, 1)
        return jnp.where(lane >= 128 - MG, v, 0.0)

    for r in range(TR):
        v = num_ref[r]
        if r < MG:
            v = v + keep_top * nu_ref[r].astype(F32)
            hl = left_of(LF, r + MG) + keep_top * left_of(UL, r + MG + TR)
            hr = right_of(RT, r + MG) + keep_top * right_of(UR, r + MG + TR)
        else:
            v = v + keep_bot * nd_ref[r - MG].astype(F32)
            hl = left_of(LF, r + MG) + keep_bot * left_of(DL, r - MG)
            hr = right_of(RT, r + MG) + keep_bot * right_of(DR, r - MG)
        v = v + jnp.concatenate([hl, hr], axis=1)
        v = v * inv_ref[r : r + 1, :]
        for half in range(2):
            scr[half, pl.ds(r, CH, stride=TR), :] = v[:, half * 128 : half * 128 + 128]
    for half in range(2):
        b_ref[:, half * 128 : half * 128 + 128] = scr[half]
    for tap in range(9):
        gm_ref[tap] = g_ref[G_MID + tap * WD : G_MID + (tap + 1) * WD].astype(F32)
        go_ref[tap] = g_ref[G_OUT + tap * CH : G_OUT + (tap + 1) * CH].astype(F32)
        gi_ref[tap] = g_ref[G_IN + tap * CH : G_IN + (tap + 1) * CH].astype(F32).T


def sds(shape, dtype):
    return jax.ShapeDtypeStruct(shape, dtype)


def shards(sizes, fields, cotangent, kernel_in, kernel_mid, kernel_out, patch_anchors, blend_weights, tile_counts):
    nla, nlo = sizes
    anch = patch_anchors[0, 0]
    dma = pltpu.SemaphoreType.DMA
    fc, edge, canv = pl.pallas_call(
        prep_kernel,
        name="prepare",
        out_shape=(sds((TR, 2 * CH, TC), BF16), sds((2 * CH, 128), BF16), sds((2 * TR, EXT), BF16)),
        in_specs=smem(2) + vmem(3),
        out_specs=vmem(3),
        scratch_shapes=[pltpu.VMEM((4, CH * TR, 128), F32)],
    )(anch, tile_counts, fields, cotangent, blend_weights)

    up, dn, en, cn = pl.pallas_call(
        functools.partial(exchange_kernel, sizes),
        name="exchange",
        out_shape=(
            sds((MG, 2 * CH, TC), BF16), sds((MG, 2 * CH, TC), BF16),
            sds((6, 2 * CH, 128), BF16), sds((8, 2 * TR, EXT), BF16),
        ),
        in_specs=vmem(3),
        out_specs=vmem(4),
        scratch_shapes=[dma((16,)), dma((16,))],
        compiler_params=pltpu.CompilerParams(collective_id=0, has_side_effects=True),
    )(fc, edge, canv)

    def two_rows(w):
        k = w.shape[1] // 3
        return jnp.concatenate([jnp.pad(w, ((0, 0), (0, k))), jnp.pad(w, ((0, 0), (k, 0)))], axis=0)

    win = two_rows(kernel_in.transpose(1, 0, 2).reshape(WD, 9 * CH))
    wmid = two_rows(kernel_mid.transpose(1, 0, 2).reshape(WD, 9 * WD))
    wout = two_rows(kernel_out.reshape(3, 3, CH, WD).transpose(1, 2, 0, 3).reshape(3 * CH, 3 * WD))
    woutt = two_rows(kernel_out[::-1].transpose(2, 0, 1).reshape(WD, 9 * CH))
    wmidt = two_rows(kernel_mid[::-1].transpose(2, 0, 1).reshape(WD, 9 * WD))

    parts = -(-(G_END // 8) // nla)
    pp = -(-parts // nlo)
    grow = nla * parts * 8
    vm = pltpu.VMEM
    num, top, bot, npk, grads, inv = pl.pallas_call(
        patch_kernel,
        name="patches",
        out_shape=(
            sds((TR, CH, TC), F32), sds((MG, CH, TC), BF16), sds((MG, CH, TC), BF16),
            sds((CH, 128), BF16), sds((grow, WD), BF16), sds((TR, TC), F32),
        ),
        in_specs=smem(2) + vmem(12),
        out_specs=vmem(6),
        scratch_shapes=[
            vm((2 * TR, 2 * CH, EXT), BF16), vm((2 * TR, EXT), F32),
            vm((3 * CH, PAD), BF16), vm((3 * CH, PAD), BF16), vm((3 * WD, PAD), BF16), vm((3 * WD, PAD), BF16),
            vm((WD, PAD), BF16), vm((WD, CELLS), F32), vm((WD, CELLS), F32), vm((WD, CELLS), BF16),
            vm((2 * TR, CH, EXT), F32), vm((3, 2 * WD, 2 * WD), F32), vm((3, 3 * CH, WD), F32), vm((3, 3 * CH, WD), F32),
        ],
    )(anch, tile_counts, fc, up, dn, en, canv, cn, blend_weights, win, wmid, wout, woutt, wmidt)

    nu, nd, n6, gs = pl.pallas_call(
        functools.partial(reduce_kernel, sizes, parts),
        name="reduce",
        out_shape=(
            sds((MG, CH, TC), BF16), sds((MG, CH, TC), BF16), sds((6, CH, 128), BF16),
            sds((nla, parts, 8, WD), BF16),
        ),
        in_specs=vmem(4),
        out_specs=vmem(4),
        scratch_shapes=[
            vm((nla, parts, 8, WD), BF16), vm((nlo, pp, 8, WD), F32), vm((parts, 8, WD), F32),
            vm((pp, 8, WD), BF16), vm((nlo * pp, 8, WD), BF16),
            dma((8,)), dma((8,)), dma((nla,)), dma((nla,)), dma((nlo,)), dma((nlo,)),
            dma((nlo,)), dma((nlo,)), dma((nla,)), dma((nla,)),
        ],
        compiler_params=pltpu.CompilerParams(collective_id=1, has_side_effects=True),
    )(top, bot, npk, grads.reshape(nla, parts, 8, WD))

    blended, gi, gm, go = pl.pallas_call(
        finish_kernel,
        name="finish",
        out_shape=(
            sds((CH * TR, TC), F32), sds((9, WD, CH), F32), sds((9, WD, WD), F32), sds((9, CH, WD), F32),
        ),
        in_specs=vmem(6),
        out_specs=vmem(4),
        scratch_shapes=[vm((2, CH * TR, 128), F32)],
    )(num, inv, nu, nd, n6, gs.reshape(grow, WD))
    return blended.reshape(CH, TR, TC), gi, gm, go


def solution(mesh):
    sizes = (mesh.shape["lat"], mesh.shape["lon"])
    return jax.shard_map(
        functools.partial(shards, sizes),
        mesh=mesh,
        in_specs=(
            P(None, "lat", "lon"), P(None, "lat", "lon"), P(), P(), P(),
            P("lat", "lon", None, None), P(None, "lat", "lon"), P("lat", "lon"),
        ),
        out_specs=(P(None, "lat", "lon"), P(), P(), P()),
        check_vma=False,
    )
```

```python
import functools

import jax
import jax.numpy as jnp
from jax import lax
from jax.experimental import pallas as pl
from jax.experimental.pallas import tpu as pltpu
from jax.sharding import PartitionSpec as P

MESH = pl.DeviceIdType.MESH
F32 = jnp.float32
BF16 = jnp.bfloat16

CH = 32
WD = 128
TR = 8
TC = 256
MG = 4
SLOTS = 4
EXT = 384
CELLS = TR * TC
PAD = (TR + 2) * TC

NB = ((-1, 0), (1, 0), (0, -1), (0, 1), (-1, -1), (-1, 1), (1, -1), (1, 1))
UP, DN, LF, RT, UL, UR, DL, DR = range(8)

G_MID, G_OUT, G_IN, G_END = 0, 9 * WD, 9 * WD + 9 * CH, 9 * WD + 18 * CH


def vmem(n):
    return [pl.BlockSpec(memory_space=pltpu.VMEM)] * n


def smem(n):
    return [pl.BlockSpec(memory_space=pltpu.SMEM)] * n


def lanes_of(shape):
    return lax.broadcasted_iota(jnp.int32, shape, len(shape) - 1)


def prep_kernel(anch, cnt, f_ref, c_ref, w_ref, fc_ref, e_ref, cv_ref, scr):
    for half in range(2):
        at = slice(half * 128, half * 128 + 128)
        scr[half] = f_ref[:, :, at].astype(F32).reshape(CH * TR, 128)
        scr[2 + half] = c_ref[:, :, at].astype(F32).reshape(CH * TR, 128)
    lane = lanes_of((2 * CH, 128))
    edge = jnp.zeros((2 * CH, 128), F32)
    for r in range(TR):
        piece = [scr[k, pl.ds(r, CH, stride=TR), :] for k in range(4)]
        row = jnp.concatenate(
            [jnp.concatenate(piece[:2], axis=1), jnp.concatenate(piece[2:], axis=1)], axis=0
        )
        fc_ref[r] = row.astype(BF16)
        first = pltpu.roll(row[:, :128], MG * r, 1) if r else row[:, :128]
        edge = jnp.where((lane >= MG * r) & (lane < MG * (r + 1)), first, edge)
        at = 32 + MG * r
        last = pltpu.roll(row[:, 128:], (at - (128 - MG)) % 128, 1)
        edge = jnp.where((lane >= at) & (lane < at + MG), last, edge)
    e_ref[...] = edge.astype(BF16)
    total = jnp.zeros((2 * TR, EXT), F32)
    for q in range(SLOTS):
        live = jnp.where(q < cnt[0, 0], 1.0, 0.0).astype(F32)
        w = w_ref[q].astype(F32) * live
        w = jnp.concatenate([w, jnp.zeros((TR, 128), F32)], axis=1)
        w = pltpu.roll(w, lax.rem(anch[1, q] + (EXT - MG), EXT), 1)
        w = jnp.concatenate([w, jnp.zeros((TR, EXT), F32)], axis=0)
        total = total + pltpu.roll(w, anch[0, q], 0)
    cv_ref[...] = total.astype(BF16)


def two_rows(a):
    k = a.shape[0] // 3
    z = jnp.zeros((k, a.shape[1]), a.dtype)
    return jnp.concatenate([a, z], axis=0), jnp.concatenate([z, a], axis=0)


def lay_weights(ki_ref, km_ref, ko_ref, win_ref, wmid_ref, wout_ref, woutt_ref, wmidt_ref):
    for dst, taps in (
        (win_ref, [ki_ref[t] for t in range(9)]),
        (woutt_ref, [ko_ref[8 - t] for t in range(9)]),
    ):
        one, two = two_rows(jnp.concatenate(taps, axis=0))
        dst[0:WD] = one.T
        dst[WD : 2 * WD] = two.T
    zero = jnp.zeros((WD, 3 * WD), BF16)
    for dst in (wmid_ref, wmidt_ref):
        dst[0:WD, 9 * WD :] = zero
        dst[WD : 2 * WD, : 3 * WD] = zero
    for t in range(9):
        for dst, w in ((wmid_ref, km_ref[t]), (wmidt_ref, km_ref[8 - t].T)):
            dst[0:WD, t * WD : (t + 1) * WD] = w
            dst[WD : 2 * WD, (t + 3) * WD : (t + 4) * WD] = w
    zero = jnp.zeros((CH, WD), BF16)
    for ro in range(2):
        for dx in range(3):
            for j in range(4):
                w = ko_ref[3 * (j - ro) + dx] if 0 <= j - ro <= 2 else zero
                at = (ro * 3 + dx) * CH
                wout_ref[at : at + CH, j * WD : (j + 1) * WD] = w


def exchange_kernel(
    sizes, fc_ref, e_ref, cv_ref, ki_ref, km_ref, ko_ref, up_ref, dn_ref, en_ref, cn_ref,
    win_ref, wmid_ref, wout_ref, woutt_ref, wmidt_ref, ssem, rsem,
):
    la, lo = lax.axis_index("lat"), lax.axis_index("lon")
    nla, nlo = sizes
    where = [(lax.rem(la + di + nla, nla), lax.rem(lo + dj + nlo, nlo)) for di, dj in NB]
    barrier = pltpu.get_barrier_semaphore()
    for dev in where:
        pl.semaphore_signal(barrier, inc=1, device_id=dev, device_id_type=MESH)
    pl.semaphore_wait(barrier, len(NB))
    copies = []

    def send(src, dst, dev, k):
        copy = pltpu.make_async_remote_copy(
            src_ref=src, dst_ref=dst, send_sem=ssem.at[k], recv_sem=rsem.at[k],
            device_id=dev, device_id_type=MESH,
        )
        copy.start()
        copies.append(copy)

    send(fc_ref.at[0:MG], dn_ref, where[UP], 0)
    send(fc_ref.at[MG:TR], up_ref, where[DN], 1)
    for k, (di, dj) in enumerate(NB):
        back = NB.index((-di, -dj))
        send(cv_ref, cn_ref.at[back], where[k], 2 + back)
        if dj:
            send(e_ref, en_ref.at[back - 2], where[k], 10 + back - 2)
    lay_weights(ki_ref, km_ref, ko_ref, win_ref, wmid_ref, wout_ref, woutt_ref, wmidt_ref)
    for copy in copies:
        copy.wait()


def shift_cols(x, step):
    lane = lanes_of((x.shape[0], 128))
    lo, hi = x[:, :128], x[:, 128:]
    zero = jnp.zeros_like(lo)
    if step < 0:
        lo, hi = pltpu.roll(lo, 1, 1), pltpu.roll(hi, 1, 1)
        return jnp.concatenate([jnp.where(lane == 0, zero, lo), jnp.where(lane == 0, lo, hi)], axis=1)
    lo, hi = pltpu.roll(lo, 127, 1), pltpu.roll(hi, 127, 1)
    return jnp.concatenate([jnp.where(lane == 127, hi, lo), jnp.where(lane == 127, zero, hi)], axis=1)


def put_shifted(buf, r, x, ch):
    at = slice((r + 1) * TC, (r + 2) * TC)
    buf[0:ch, at] = shift_cols(x, -1)
    buf[ch : 2 * ch, at] = x
    buf[2 * ch : 3 * ch, at] = shift_cols(x, 1)


def four_rows(buf, i, rows=slice(None)):
    return jnp.concatenate([buf[rows, (2 * i + j) * TC : (2 * i + j + 1) * TC] for j in range(4)], axis=0)


def dot(a, b):
    return jnp.dot(a, b, preferred_element_type=F32)


def dot_t(a, b):
    return lax.dot_general(a, b, (((1,), (1,)), ((), ())), preferred_element_type=F32)


def patch_kernel(
    anch, cnt, fc_ref, up_ref, dn_ref, en_ref, cv_ref, cn_ref, w_ref, win_ref, wmid_ref, wout_ref,
    woutt_ref, wmidt_ref, num_ref, top_ref, bot_ref, np_ref, g_ref, inv_ref,
    ext, inv, xpb, dpb, h1b, dzb, h2b, sl1, dh2, dz1, canvas, gmid, gout, gin,
):
    la, nla = lax.axis_index("lat"), lax.axis_size("lat")
    keep_top = la > 0
    keep_bot = la < nla - 1

    lane = lanes_of((2 * TR, EXT))
    den = cv_ref[...].astype(F32)

    def rows_of(k, canv):
        di = NB[k][0]
        zero = jnp.zeros((TR, EXT), F32)
        if di < 0:
            part = jnp.where(keep_top, canv[TR:], zero)
            return jnp.concatenate([part, zero], axis=0)
        if di > 0:
            part = jnp.where(keep_bot, canv[:TR], zero)
            return jnp.concatenate([zero, part], axis=0)
        return canv

    for k, (di, dj) in enumerate(NB):
        canv = cn_ref[k].astype(F32)
        if dj > 0:
            canv = jnp.concatenate([canv[:, 128:], canv[:, :128]], axis=1)
            canv = jnp.where((lane >= TC - MG) & (lane < TC + MG), canv, 0.0)
        if dj < 0:
            canv = jnp.concatenate([canv[:, 256:], canv[:, :256]], axis=1)
            canv = jnp.where((lane >= EXT - MG) | (lane < MG), canv, 0.0)
        den = den + rows_of(k, canv)
    inv[...] = 1.0 / jnp.maximum(den, 1.0)
    inv_ref[...] = inv[MG : MG + TR, :TC]

    hl = lanes_of((2 * CH, 128))
    for t in range(2 * TR):
        if t < MG:
            center, left, right, r, keep = up_ref[t], UL, UR, t + MG, keep_top
        elif t < MG + TR:
            center, left, right, r, keep = fc_ref[t - MG], LF, RT, t - MG, None
        else:
            center, left, right, r, keep = dn_ref[t - MG - TR], DL, DR, t - MG - TR, keep_bot
        lp = pltpu.roll(en_ref[left - 2].astype(F32), (96 - MG - MG * r) % 128, 1)
        rp = en_ref[right - 2].astype(F32)
        rp = pltpu.roll(rp, 128 - MG * r, 1) if r else rp
        row = jnp.concatenate([center.astype(F32), jnp.where(hl < 64, rp, lp)], axis=1)
        if keep is not None:
            row = jnp.where(keep, row, 0.0)
        ext[t, 0:CH, :] = row[:CH].astype(BF16)
        ext[t, CH:, :] = (row[CH:] * inv[t : t + 1, :]).astype(BF16)

    for buf in (xpb, dpb, h1b, dzb, h2b):
        z = jnp.zeros((buf.shape[0], TC), BF16)
        buf[:, 0:TC] = z
        buf[:, PAD - TC : PAD] = z
    canvas[...] = jnp.zeros_like(canvas)
    gmid[...] = jnp.zeros_like(gmid)
    gout[...] = jnp.zeros_like(gout)
    gin[...] = jnp.zeros_like(gin)

    def one_patch(q, carry):
        a, b = anch[0, q], anch[1, q]
        turn = lax.rem(EXT + MG - b, EXT)
        place = lax.rem(b + (EXT - MG), EXT)
        weights = w_ref[q].astype(F32)

        def rows(i):
            return range(2 * i, 2 * i + 2)

        def at(r):
            return slice(r * TC, (r + 1) * TC)

        def half(z, r):
            n = z.shape[0] // 2
            return z[:n] if r % 2 == 0 else z[n:]

        def window(i):
            for r in rows(i):
                x = pltpu.roll(ext[a + r].astype(F32), turn, 1)[:, :TC]
                put_shifted(xpb, r, x[:CH].astype(BF16), CH)
                put_shifted(dpb, r, (x[CH:] * weights[r : r + 1, :]).astype(BF16), CH)

        def first(i):
            zz = dot(win_ref[...], four_rows(xpb, i))
            for r in rows(i):
                z = half(zz, r)
                t = jnp.tanh(0.5 * z)
                s = 0.5 + 0.5 * t
                h = z * s
                put_shifted(h1b, r, h.astype(BF16), WD)
                sl1[:, at(r)] = s + h * (1.0 - s)

        def second(i):
            zz = dot(wmid_ref[...], four_rows(h1b, i))
            gg = dot(woutt_ref[...], four_rows(dpb, i))
            for r in rows(i):
                z, g = half(zz, r), half(gg, r)
                t = jnp.tanh(0.5 * z)
                s = 0.5 + 0.5 * t
                h = z * s
                h2b[:, at(r + 1)] = (h1b[WD : 2 * WD, at(r + 1)].astype(F32) + h).astype(BF16)
                dh2[:, at(r)] = g
                put_shifted(dzb, r, (g * (s + h * (1.0 - s))).astype(BF16), WD)

        def blend(i):
            oo = dot(wout_ref[...], four_rows(h2b, i))
            for r in rows(i):
                v = half(oo, r)
                o = shift_cols(v[0:CH], -1) + v[CH : 2 * CH] + shift_cols(v[2 * CH :], 1)
                o = o * weights[r : r + 1, :]
                o = jnp.concatenate([o, jnp.zeros((CH, 128), F32)], axis=1)
                canvas[a + r] += pltpu.roll(o, place, 1)

        def third(i):
            zz = dot(wmidt_ref[...], four_rows(dzb, i))
            for r in rows(i):
                g = dh2[:, at(r)] + half(zz, r)
                dz1[:, at(r)] = (g * sl1[:, at(r)]).astype(BF16)

        window(0)
        window(1)
        first(0)
        window(2)
        first(1)
        window(3)
        second(0)
        first(2)
        second(1)
        first(3)
        third(0)
        blend(0)
        second(2)
        third(1)
        blend(1)
        second(3)
        third(2)
        blend(2)
        third(3)
        blend(3)

        hh = h2b[:, TC : TC + CELLS]
        d1 = dz1[...]
        d2 = dzb[0 : 2 * WD, TC : TC + CELLS]
        for dy in range(3):
            gmid[dy] += dot_t(d2, h1b[0 : 2 * WD, dy * TC : dy * TC + CELLS])
            gout[dy] += dot_t(dpb[:, (2 - dy) * TC : (2 - dy) * TC + CELLS], hh)
            gin[dy] += dot_t(xpb[:, dy * TC : dy * TC + CELLS], d1)
        return carry

    lax.fori_loop(0, cnt[0, 0], one_patch, 0)

    for r in range(TR):
        num_ref[r] = canvas[MG + r, :, :TC]
    for r in range(MG):
        top_ref[r] = canvas[r, :, :TC].astype(BF16)
        bot_ref[r] = canvas[MG + TR + r, :, :TC].astype(BF16)
    pk_lane = lanes_of((CH, 128))
    pk = jnp.zeros((CH, 128), F32)
    for t in range(2 * TR):
        v = canvas[t, :, TC:]
        hi = pltpu.roll(v, MG * t, 1) if t else v
        pk = jnp.where((pk_lane >= MG * t) & (pk_lane < MG * (t + 1)), hi, pk)
        at = 64 + MG * t
        lo = pltpu.roll(v, (at - (128 - MG)) % 128, 1)
        pk = jnp.where((pk_lane >= at) & (pk_lane < at + MG), lo, pk)
    np_ref[...] = pk.astype(BF16)
    for tap in range(9):
        dy, dx = divmod(tap, 3)
        ro, co = ((1, 0), (1, 1), (0, 1))[dx]
        g_ref[G_MID + tap * WD : G_MID + (tap + 1) * WD] = gmid[
            dy, ro * WD : (ro + 1) * WD, co * WD : (co + 1) * WD
        ]
        s = 2 - dx
        g_ref[G_OUT + tap * CH : G_OUT + (tap + 1) * CH] = gout[dy, s * CH : (s + 1) * CH]
        g_ref[G_IN + tap * CH : G_IN + (tap + 1) * CH] = gin[dy, dx * CH : (dx + 1) * CH]
    if g_ref.shape[0] > G_END:
        g_ref[G_END:] = jnp.zeros((g_ref.shape[0] - G_END, WD), F32)


class Place:
    def __init__(self, dims):
        self.dims = dims
        yl, x, yh, z = dims
        self.chips, self.depth = yh * yl * x, z
        self.la, self.lo = lax.axis_index("lat"), lax.axis_index("lon")
        self.core = lax.rem(self.la, 2)
        self.z = lax.rem(self.lo, z)
        self.chip = ((self.lo // z) * yl + self.la // (2 * x)) * x + lax.rem(self.la // 2, x)

    def in_plane(self, k):
        yl, x, yh, z = self.dims
        chip = lax.rem(self.chip + k, self.chips)
        y = chip // x
        la = (lax.rem(y, yl) * x + lax.rem(chip, x)) * 2 + self.core
        return chip, (la, (y // yl) * z + self.z)

    def sibling(self):
        return (self.la + 1 - 2 * self.core, self.lo)

    def along_z(self, k):
        z = lax.rem(self.z + k, self.depth)
        return z, (self.la, self.lo - self.z + z)


def copy_to(src, dst, ss, rs, dev):
    return pltpu.make_async_remote_copy(
        src_ref=src, dst_ref=dst, send_sem=ss, recv_sem=rs, device_id=dev, device_id_type=MESH
    )


def greet(place, sizes):
    barrier = pltpu.get_barrier_semaphore()
    nla, nlo = sizes
    where = [(lax.rem(place.la + di + nla, nla), lax.rem(place.lo + dj + nlo, nlo)) for di, dj in NB]
    devs = where + [place.sibling()]
    devs += [place.in_plane(k)[1] for k in range(1, place.chips)]
    devs += [place.along_z(k)[1] for k in range(1, place.depth)]
    for dev in devs:
        pl.semaphore_signal(barrier, inc=1, device_id=dev, device_id_type=MESH)
    return where, barrier, len(devs)


def send_edges(where, top_ref, bot_ref, np_ref, nu_ref, nd_ref, n6_ref, ssem, rsem):
    edges = [
        copy_to(top_ref, nd_ref, ssem.at[0], rsem.at[0], where[UP]),
        copy_to(bot_ref, nu_ref, ssem.at[1], rsem.at[1], where[DN]),
    ]
    for k, (di, dj) in enumerate(NB):
        if dj:
            back = NB.index((-di, -dj)) - 2
            edges.append(copy_to(np_ref, n6_ref.at[back], ssem.at[2 + back], rsem.at[2 + back], where[k]))
    for c in edges:
        c.start()
    return edges


def sum_devices(place, g_ref, gs_ref, pair, rel, got, zs, zb, fin, sems):
    n, depth, core = place.chips, place.depth, place.core
    other = 1 - core
    s0, r0, s1, r1, s2, r2, s3, r3, s4, r4 = sems
    sib = place.sibling()
    order = list(range(1, n)) + [0]

    sent = []
    for k in order:
        chip, _ = place.in_plane(k)
        c = copy_to(g_ref.at[other, chip], pair.at[k], s0.at[k], r0.at[k], sib)
        c.start()
        sent.append(c)
    mine = None
    for k in order:
        chip, dev = place.in_plane(k)
        copy_to(g_ref.at[0, 0], pair.at[k], s0.at[k], r0.at[k], sib).wait_recv()
        both = g_ref[core, chip] + pair[k]
        if k:
            rel[k] = both.astype(BF16)
            c = copy_to(rel.at[k], got.at[n - k], s1.at[k], r1.at[n - k], dev)
            c.start()
            sent.append(c)
        else:
            mine = both
    for k in range(1, n):
        copy_to(rel.at[k], got.at[k], s1.at[k], r1.at[k], sib).wait_recv()
        mine = mine + got[k].astype(F32)
    zs[...] = mine.astype(BF16)
    for k in range(1, depth):
        _, dev = place.along_z(k)
        c = copy_to(zs, zb.at[place.z], s2.at[k], r2.at[depth - k], dev)
        c.start()
        sent.append(c)
    zb[place.z] = zs[...]
    for k in range(1, depth):
        z, _ = place.along_z(k)
        copy_to(zs, zb.at[z], s2.at[k], r2.at[k], sib).wait_recv()
    total = zb[0].astype(F32)
    for z in range(1, depth):
        total = total + zb[z].astype(F32)
    fin[...] = total.astype(BF16)
    for k in range(1, n):
        _, dev = place.in_plane(k)
        c = copy_to(fin, gs_ref.at[core, place.chip], s3.at[k], r3.at[n - k], dev)
        c.start()
        sent.append(c)
    c = copy_to(fin, gs_ref.at[core, place.chip], s4.at[0], r4.at[0], sib)
    c.start()
    sent.append(c)
    gs_ref[core, place.chip] = fin[...]
    for k in range(1, n):
        chip, _ = place.in_plane(k)
        copy_to(fin, gs_ref.at[core, chip], s3.at[k], r3.at[k], sib).wait_recv()
        c = copy_to(gs_ref.at[core, chip], gs_ref.at[core, chip], s4.at[k], r4.at[k], sib)
        c.start()
        sent.append(c)
    for k in range(n):
        chip, _ = place.in_plane(k)
        copy_to(fin, gs_ref.at[other, chip], s4.at[k], r4.at[k], sib).wait_recv()
    return sent


def sum_scratch(dims, rows):
    yl, x, yh, z = dims
    n = yl * x * yh
    part = (rows, WD)
    dma = pltpu.SemaphoreType.DMA
    bufs = [pltpu.VMEM((n,) + part, F32)] + [pltpu.VMEM((n,) + part, BF16)] * 2
    bufs += [pltpu.VMEM(part, BF16), pltpu.VMEM((z,) + part, BF16), pltpu.VMEM(part, BF16)]
    return bufs + [dma((m,)) for m in (n, n, n, n, z, z, n, n, n, n)]


def reduce_kernel(sizes, dims, top_ref, bot_ref, np_ref, g_ref, nu_ref, nd_ref, n6_ref, gs_ref, ssem, rsem, *rest):
    place = Place(dims)
    where, barrier, n = greet(place, sizes)
    pl.semaphore_wait(barrier, n)
    edges = send_edges(where, top_ref, bot_ref, np_ref, nu_ref, nd_ref, n6_ref, ssem, rsem)
    sent = sum_devices(place, g_ref, gs_ref, *rest[:6], rest[6:])
    for c in edges:
        c.wait_recv()
    for c in edges + sent:
        c.wait_send()


def finish_kernel(num_ref, inv_ref, nu_ref, nd_ref, n6_ref, g_ref, b_ref, gi_ref, gm_ref, go_ref, scr):
    la, nla = lax.axis_index("lat"), lax.axis_size("lat")
    keep_top = jnp.where(la > 0, 1.0, 0.0).astype(F32)
    keep_bot = jnp.where(la < nla - 1, 1.0, 0.0).astype(F32)
    lane = lanes_of((CH, 128))

    def left_of(k, t):
        v = pltpu.roll(n6_ref[k - 2].astype(F32), (128 - MG * t) % 128, 1) if t else n6_ref[k - 2].astype(F32)
        return jnp.where(lane < MG, v, 0.0)

    def right_of(k, t):
        v = pltpu.roll(n6_ref[k - 2].astype(F32), (64 - MG - MG * t) % 128, 1)
        return jnp.where(lane >= 128 - MG, v, 0.0)

    for r in range(TR):
        v = num_ref[r]
        if r < MG:
            v = v + keep_top * nu_ref[r].astype(F32)
            hl = left_of(LF, r + MG) + keep_top * left_of(UL, r + MG + TR)
            hr = right_of(RT, r + MG) + keep_top * right_of(UR, r + MG + TR)
        else:
            v = v + keep_bot * nd_ref[r - MG].astype(F32)
            hl = left_of(LF, r + MG) + keep_bot * left_of(DL, r - MG)
            hr = right_of(RT, r + MG) + keep_bot * right_of(DR, r - MG)
        v = v + jnp.concatenate([hl, hr], axis=1)
        v = v * inv_ref[r : r + 1, :]
        for half in range(2):
            scr[half, pl.ds(r, CH, stride=TR), :] = v[:, half * 128 : half * 128 + 128]
    for half in range(2):
        b_ref[:, half * 128 : half * 128 + 128] = scr[half]
    for tap in range(9):
        gm_ref[tap] = g_ref[G_MID + tap * WD : G_MID + (tap + 1) * WD].astype(F32)
        go_ref[tap] = g_ref[G_OUT + tap * CH : G_OUT + (tap + 1) * CH].astype(F32)
        gi_ref[tap] = g_ref[G_IN + tap * CH : G_IN + (tap + 1) * CH].astype(F32)


def sds(shape, dtype):
    return jax.ShapeDtypeStruct(shape, dtype)


def shards(sizes, fields, cotangent, kernel_in, kernel_mid, kernel_out, patch_anchors, blend_weights, tile_counts):
    nla, nlo = sizes
    anch = patch_anchors.transpose(0, 1, 3, 2)[0, 0]
    dma = pltpu.SemaphoreType.DMA
    fc, edge, canv = pl.pallas_call(
        prep_kernel,
        name="prepare",
        out_shape=(sds((TR, 2 * CH, TC), BF16), sds((2 * CH, 128), BF16), sds((2 * TR, EXT), BF16)),
        in_specs=smem(2) + vmem(3),
        out_specs=vmem(3),
        scratch_shapes=[pltpu.VMEM((4, CH * TR, 128), F32)],
    )(anch, tile_counts, fields, cotangent, blend_weights)

    up, dn, en, cn, win, wmid, wout, woutt, wmidt = pl.pallas_call(
        functools.partial(exchange_kernel, sizes),
        name="exchange",
        out_shape=(
            sds((MG, 2 * CH, TC), BF16), sds((MG, 2 * CH, TC), BF16),
            sds((6, 2 * CH, 128), BF16), sds((8, 2 * TR, EXT), BF16),
            sds((2 * WD, 12 * CH), BF16), sds((2 * WD, 12 * WD), BF16), sds((6 * CH, 4 * WD), BF16),
            sds((2 * WD, 12 * CH), BF16), sds((2 * WD, 12 * WD), BF16),
        ),
        in_specs=vmem(6),
        out_specs=vmem(9),
        scratch_shapes=[dma((16,)), dma((16,))],
        compiler_params=pltpu.CompilerParams(collective_id=0, has_side_effects=True),
    )(fc, edge, canv, kernel_in.transpose(0, 2, 1), kernel_mid, kernel_out)

    dims = (2, 4, 2, 8) if sizes == (16, 16) else (1, nla // 2, 1, nlo)
    parts = dims[0] * dims[1] * dims[2]
    rows = -(-G_END // (16 * parts)) * 8
    grow = 2 * parts * rows
    vm = pltpu.VMEM
    num, top, bot, npk, grads, inv = pl.pallas_call(
        patch_kernel,
        name="patches",
        out_shape=(
            sds((TR, CH, TC), F32), sds((MG, CH, TC), BF16), sds((MG, CH, TC), BF16),
            sds((CH, 128), BF16), sds((grow, WD), F32), sds((TR, TC), F32),
        ),
        in_specs=smem(2) + vmem(12),
        out_specs=vmem(6),
        scratch_shapes=[
            vm((2 * TR, 2 * CH, EXT), BF16), vm((2 * TR, EXT), F32),
            vm((3 * CH, PAD), BF16), vm((3 * CH, PAD), BF16), vm((3 * WD, PAD), BF16), vm((3 * WD, PAD), BF16),
            vm((WD, PAD), BF16), vm((WD, CELLS), F32), vm((WD, CELLS), F32), vm((WD, CELLS), BF16),
            vm((2 * TR, CH, EXT), F32), vm((3, 2 * WD, 2 * WD), F32), vm((3, 3 * CH, WD), F32), vm((3, 3 * CH, WD), F32),
        ],
    )(anch, tile_counts, fc, up, dn, en, canv, cn, blend_weights, win, wmid, wout, woutt, wmidt)

    nu, nd, n6, gs = pl.pallas_call(
        functools.partial(reduce_kernel, sizes, dims),
        name="reduce",
        out_shape=(
            sds((MG, CH, TC), BF16), sds((MG, CH, TC), BF16), sds((6, CH, 128), BF16),
            sds((2, parts, rows, WD), BF16),
        ),
        in_specs=vmem(4),
        out_specs=vmem(4),
        scratch_shapes=[dma((8,)), dma((8,))] + sum_scratch(dims, rows),
        compiler_params=pltpu.CompilerParams(collective_id=1, has_side_effects=True),
    )(top, bot, npk, grads.reshape(2, parts, rows, WD))

    blended, gi, gm, go = pl.pallas_call(
        finish_kernel,
        name="finish",
        out_shape=(
            sds((CH * TR, TC), F32), sds((9, CH, WD), F32), sds((9, WD, WD), F32), sds((9, CH, WD), F32),
        ),
        in_specs=vmem(6),
        out_specs=vmem(4),
        scratch_shapes=[vm((2, CH * TR, 128), F32)],
    )(num, inv, nu, nd, n6, gs.reshape(grow, WD))
    return blended.reshape(CH, TR, TC), gi.transpose(0, 2, 1), gm, go


def solution(mesh):
    sizes = (mesh.shape["lat"], mesh.shape["lon"])
    return jax.shard_map(
        functools.partial(shards, sizes),
        mesh=mesh,
        in_specs=(
            P(None, "lat", "lon"), P(None, "lat", "lon"), P(), P(), P(),
            P("lat", "lon", None, None), P(None, "lat", "lon"), P("lat", "lon"),
        ),
        out_specs=(P(None, "lat", "lon"), P(), P(), P()),
        check_vma=False,
    )
```

```python
import functools

import jax
import jax.numpy as jnp
from jax import lax
from jax.experimental import pallas as pl
from jax.experimental.pallas import tpu as pltpu
from jax.sharding import PartitionSpec as P

MESH = pl.DeviceIdType.MESH
F32 = jnp.float32
BF16 = jnp.bfloat16

CH = 32
WD = 128
TR = 8
TC = 256
MG = 4
SLOTS = 4
EXT = 384
CELLS = TR * TC
PAD = (TR + 2) * TC

NB = ((-1, 0), (1, 0), (0, -1), (0, 1), (-1, -1), (-1, 1), (1, -1), (1, 1))
UP, DN, LF, RT, UL, UR, DL, DR = range(8)

G_MID, G_OUT, G_IN, G_END = 0, 9 * WD, 9 * WD + 9 * CH, 9 * WD + 18 * CH


def vmem(n):
    return [pl.BlockSpec(memory_space=pltpu.VMEM)] * n


def smem(n):
    return [pl.BlockSpec(memory_space=pltpu.SMEM)] * n


def lanes_of(shape):
    return lax.broadcasted_iota(jnp.int32, shape, len(shape) - 1)


def prepare(anch, cnt, f_ref, c_ref, w_ref, fc_ref, e_ref, cv_ref, scr):
    for half in range(2):
        at = slice(half * 128, half * 128 + 128)
        scr[half] = f_ref[:, :, at].astype(F32).reshape(CH * TR, 128)
        scr[2 + half] = c_ref[:, :, at].astype(F32).reshape(CH * TR, 128)
    lane = lanes_of((2 * CH, 128))
    edge = jnp.zeros((2 * CH, 128), F32)
    for r in range(TR):
        piece = [scr[k, pl.ds(r, CH, stride=TR), :] for k in range(4)]
        row = jnp.concatenate(
            [jnp.concatenate(piece[:2], axis=1), jnp.concatenate(piece[2:], axis=1)], axis=0
        )
        fc_ref[r] = row.astype(BF16)
        first = pltpu.roll(row[:, :128], MG * r, 1) if r else row[:, :128]
        edge = jnp.where((lane >= MG * r) & (lane < MG * (r + 1)), first, edge)
        at = 32 + MG * r
        last = pltpu.roll(row[:, 128:], (at - (128 - MG)) % 128, 1)
        edge = jnp.where((lane >= at) & (lane < at + MG), last, edge)
    e_ref[...] = edge.astype(BF16)
    total = jnp.zeros((2 * TR, EXT), F32)
    for q in range(SLOTS):
        live = jnp.where(q < cnt[0, 0], 1.0, 0.0).astype(F32)
        w = w_ref[q].astype(F32) * live
        w = jnp.concatenate([w, jnp.zeros((TR, 128), F32)], axis=1)
        w = pltpu.roll(w, lax.rem(anch[1, q] + (EXT - MG), EXT), 1)
        w = jnp.concatenate([w, jnp.zeros((TR, EXT), F32)], axis=0)
        total = total + pltpu.roll(w, anch[0, q], 0)
    cv_ref[...] = total.astype(BF16)


def two_rows(a):
    k = a.shape[0] // 3
    z = jnp.zeros((k, a.shape[1]), a.dtype)
    return jnp.concatenate([a, z], axis=0), jnp.concatenate([z, a], axis=0)


def lay_weights(ki_ref, km_ref, ko_ref, win_ref, wmid_ref, wout_ref, woutt_ref, wmidt_ref):
    for dst, taps in (
        (win_ref, [ki_ref[t] for t in range(9)]),
        (woutt_ref, [ko_ref[8 - t] for t in range(9)]),
    ):
        one, two = two_rows(jnp.concatenate(taps, axis=0))
        dst[0:WD] = one.T
        dst[WD : 2 * WD] = two.T
    for t in range(9):
        wmid_ref[:, t * WD : (t + 1) * WD] = km_ref[t]
        wmidt_ref[:, t * WD : (t + 1) * WD] = km_ref[8 - t].T
    zero = jnp.zeros((CH, WD), BF16)
    for ro in range(2):
        for dx in range(3):
            for j in range(4):
                w = ko_ref[3 * (j - ro) + dx] if 0 <= j - ro <= 2 else zero
                at = (ro * 3 + dx) * CH
                wout_ref[at : at + CH, j * WD : (j + 1) * WD] = w


def exchange_kernel(
    sizes, anch, cnt, f_ref, c_ref, w_ref, ki_ref, km_ref, ko_ref, fc_ref, cv_ref, up_ref, dn_ref, en_ref, cn_ref,
    win_ref, wmid_ref, wout_ref, woutt_ref, wmidt_ref, e_ref, scr, ssem, rsem,
):
    la, lo = lax.axis_index("lat"), lax.axis_index("lon")
    nla, nlo = sizes
    where = [(lax.rem(la + di + nla, nla), lax.rem(lo + dj + nlo, nlo)) for di, dj in NB]
    barrier = pltpu.get_barrier_semaphore()
    for dev in where:
        pl.semaphore_signal(barrier, inc=1, device_id=dev, device_id_type=MESH)
    prepare(anch, cnt, f_ref, c_ref, w_ref, fc_ref, e_ref, cv_ref, scr)
    pl.semaphore_wait(barrier, len(NB))
    copies = []

    def send(src, dst, dev, k):
        copy = pltpu.make_async_remote_copy(
            src_ref=src, dst_ref=dst, send_sem=ssem.at[k], recv_sem=rsem.at[k],
            device_id=dev, device_id_type=MESH,
        )
        copy.start()
        copies.append(copy)

    send(fc_ref.at[0:MG], dn_ref, where[UP], 0)
    send(fc_ref.at[MG:TR], up_ref, where[DN], 1)
    for k, (di, dj) in enumerate(NB):
        back = NB.index((-di, -dj))
        send(cv_ref, cn_ref.at[back], where[k], 2 + back)
        if dj:
            send(e_ref, en_ref.at[back - 2], where[k], 10 + back - 2)
    lay_weights(ki_ref, km_ref, ko_ref, win_ref, wmid_ref, wout_ref, woutt_ref, wmidt_ref)
    for copy in copies:
        copy.wait()


def shift_cols(x, step):
    lane = lanes_of((x.shape[0], 128))
    lo, hi = x[:, :128], x[:, 128:]
    zero = jnp.zeros_like(lo)
    if step < 0:
        lo, hi = pltpu.roll(lo, 1, 1), pltpu.roll(hi, 1, 1)
        return jnp.concatenate([jnp.where(lane == 0, zero, lo), jnp.where(lane == 0, lo, hi)], axis=1)
    lo, hi = pltpu.roll(lo, 127, 1), pltpu.roll(hi, 127, 1)
    return jnp.concatenate([jnp.where(lane == 127, hi, lo), jnp.where(lane == 127, zero, hi)], axis=1)


def put_shifted(buf, r, x, ch):
    at = slice((r + 1) * TC, (r + 2) * TC)
    buf[0:ch, at] = shift_cols(x, -1)
    buf[ch : 2 * ch, at] = x
    buf[2 * ch : 3 * ch, at] = shift_cols(x, 1)


def put_two(buf, r, x, ch):
    at = slice((r + 1) * TC, (r + 2) * TC)
    buf[0:ch, at] = shift_cols(x, -1)
    buf[ch : 2 * ch, at] = x


def four_rows(buf, i, rows=slice(None)):
    return jnp.concatenate([buf[rows, (2 * i + j) * TC : (2 * i + j + 1) * TC] for j in range(4)], axis=0)


def three_rows(buf, r):
    return jnp.concatenate([buf[:, (r + j) * TC : (r + j + 1) * TC] for j in range(3)], axis=0)


def dot(a, b):
    return jnp.dot(a, b, preferred_element_type=F32)


def dot_t(a, b):
    return lax.dot_general(a, b, (((1,), (1,)), ((), ())), preferred_element_type=F32)


def patch_kernel(
    anch, cnt, fc_ref, up_ref, dn_ref, en_ref, cv_ref, cn_ref, w_ref, win_ref, wmid_ref, wout_ref,
    woutt_ref, wmidt_ref, num_ref, top_ref, bot_ref, np_ref, g_ref, inv_ref,
    ext, inv, xpb, dpb, h1b, dzb, h2b, sl1, dh2, dz1, canvas, gmid, gout, gin,
):
    la, nla = lax.axis_index("lat"), lax.axis_size("lat")
    keep_top = la > 0
    keep_bot = la < nla - 1

    lane = lanes_of((2 * TR, EXT))
    den = cv_ref[...].astype(F32)

    def rows_of(k, canv):
        di = NB[k][0]
        zero = jnp.zeros((TR, EXT), F32)
        if di < 0:
            part = jnp.where(keep_top, canv[TR:], zero)
            return jnp.concatenate([part, zero], axis=0)
        if di > 0:
            part = jnp.where(keep_bot, canv[:TR], zero)
            return jnp.concatenate([zero, part], axis=0)
        return canv

    for k, (di, dj) in enumerate(NB):
        canv = cn_ref[k].astype(F32)
        if dj > 0:
            canv = jnp.concatenate([canv[:, 128:], canv[:, :128]], axis=1)
            canv = jnp.where((lane >= TC - MG) & (lane < TC + MG), canv, 0.0)
        if dj < 0:
            canv = jnp.concatenate([canv[:, 256:], canv[:, :256]], axis=1)
            canv = jnp.where((lane >= EXT - MG) | (lane < MG), canv, 0.0)
        den = den + rows_of(k, canv)
    inv[...] = 1.0 / jnp.maximum(den, 1.0)
    inv_ref[...] = inv[MG : MG + TR, :TC]

    hl = lanes_of((2 * CH, 128))
    for t in range(2 * TR):
        if t < MG:
            center, left, right, r, keep = up_ref[t], UL, UR, t + MG, keep_top
        elif t < MG + TR:
            center, left, right, r, keep = fc_ref[t - MG], LF, RT, t - MG, None
        else:
            center, left, right, r, keep = dn_ref[t - MG - TR], DL, DR, t - MG - TR, keep_bot
        lp = pltpu.roll(en_ref[left - 2].astype(F32), (96 - MG - MG * r) % 128, 1)
        rp = en_ref[right - 2].astype(F32)
        rp = pltpu.roll(rp, 128 - MG * r, 1) if r else rp
        row = jnp.concatenate([center.astype(F32), jnp.where(hl < 64, rp, lp)], axis=1)
        if keep is not None:
            row = jnp.where(keep, row, 0.0)
        ext[t, 0:CH, :] = row[:CH].astype(BF16)
        ext[t, CH:, :] = (row[CH:] * inv[t : t + 1, :]).astype(BF16)

    for buf in (xpb, dpb, h1b, dzb, h2b):
        z = jnp.zeros((buf.shape[0], TC), BF16)
        buf[:, 0:TC] = z
        buf[:, PAD - TC : PAD] = z
    canvas[...] = jnp.zeros_like(canvas)
    gmid[...] = jnp.zeros_like(gmid)
    gout[...] = jnp.zeros_like(gout)
    gin[...] = jnp.zeros_like(gin)

    def one_patch(q, carry):
        a, b = anch[0, q], anch[1, q]
        turn = lax.rem(EXT + MG - b, EXT)
        place = lax.rem(b + (EXT - MG), EXT)
        weights = w_ref[q].astype(F32)

        def rows(i):
            return range(2 * i, 2 * i + 2)

        def at(r):
            return slice(r * TC, (r + 1) * TC)

        def half(z, r):
            n = z.shape[0] // 2
            return z[:n] if r % 2 == 0 else z[n:]

        def window(i):
            for r in rows(i):
                x = pltpu.roll(ext[a + r].astype(F32), turn, 1)[:, :TC]
                put_shifted(xpb, r, x[:CH].astype(BF16), CH)
                put_shifted(dpb, r, (x[CH:] * weights[r : r + 1, :]).astype(BF16), CH)

        def first(i):
            zz = dot(win_ref[...], four_rows(xpb, i))
            for r in rows(i):
                z = half(zz, r)
                t = jnp.tanh(0.5 * z)
                s = 0.5 + 0.5 * t
                h = z * s
                put_shifted(h1b, r, h.astype(BF16), WD)
                sl1[:, at(r)] = s + h * (1.0 - s)

        def second(i):
            gg = dot(woutt_ref[...], four_rows(dpb, i))
            for r in rows(i):
                z, g = dot(wmid_ref[...], three_rows(h1b, r)), half(gg, r)
                t = jnp.tanh(0.5 * z)
                s = 0.5 + 0.5 * t
                h = z * s
                put_two(h2b, r, (h1b[WD : 2 * WD, at(r + 1)].astype(F32) + h).astype(BF16), WD)
                dh2[:, at(r)] = g
                put_shifted(dzb, r, (g * (s + h * (1.0 - s))).astype(BF16), WD)

        def blend(i):
            oo = dot(wout_ref[...], four_rows(h2b, i, slice(WD, 2 * WD)))
            for r in rows(i):
                v = half(oo, r)
                o = shift_cols(v[0:CH], -1) + v[CH : 2 * CH] + shift_cols(v[2 * CH :], 1)
                o = o * weights[r : r + 1, :]
                o = jnp.concatenate([o, jnp.zeros((CH, 128), F32)], axis=1)
                canvas[a + r] += pltpu.roll(o, place, 1)

        def third(i):
            for r in rows(i):
                g = dh2[:, at(r)] + dot(wmidt_ref[...], three_rows(dzb, r))
                put_two(dz1, r, (g * sl1[:, at(r)]).astype(BF16), WD)

        window(0)
        window(1)
        first(0)
        window(2)
        first(1)
        window(3)
        second(0)
        first(2)
        second(1)
        first(3)
        third(0)
        blend(0)
        second(2)
        third(1)
        blend(1)
        second(3)
        third(2)
        blend(2)
        third(3)
        blend(3)

        def slab(buf, n, row):
            return buf[0:n, row * TC : row * TC + CELLS]

        gmid[...] += dot_t(
            dzb[WD : 2 * WD, TC : TC + CELLS],
            jnp.concatenate([slab(h1b, 3 * WD, dy) for dy in range(3)], axis=0),
        )
        gout[...] += dot_t(
            jnp.concatenate([slab(dpb, 2 * CH, 2 - dy) for dy in range(3)], axis=0), slab(h2b, 2 * WD, 1)
        )
        gin[...] += dot_t(
            jnp.concatenate([slab(xpb, 2 * CH, dy) for dy in range(3)], axis=0), slab(dz1, 2 * WD, 1)
        )
        return carry

    lax.fori_loop(0, cnt[0, 0], one_patch, 0)

    for r in range(TR):
        num_ref[r] = canvas[MG + r, :, :TC]
    for r in range(MG):
        top_ref[r] = canvas[r, :, :TC].astype(BF16)
        bot_ref[r] = canvas[MG + TR + r, :, :TC].astype(BF16)
    pk_lane = lanes_of((CH, 128))
    pk = jnp.zeros((CH, 128), F32)
    for t in range(2 * TR):
        v = canvas[t, :, TC:]
        hi = pltpu.roll(v, MG * t, 1) if t else v
        pk = jnp.where((pk_lane >= MG * t) & (pk_lane < MG * (t + 1)), hi, pk)
        at = 64 + MG * t
        lo = pltpu.roll(v, (at - (128 - MG)) % 128, 1)
        pk = jnp.where((pk_lane >= at) & (pk_lane < at + MG), lo, pk)
    np_ref[...] = pk.astype(BF16)
    for tap in range(9):
        dy, dx = divmod(tap, 3)
        g_ref[G_MID + tap * WD : G_MID + (tap + 1) * WD] = gmid[:, tap * WD : (tap + 1) * WD]
        ro, co = ((1, 0), (1, 1), (0, 1))[dx]
        at = (2 * dy + ro) * CH
        g_ref[G_OUT + tap * CH : G_OUT + (tap + 1) * CH] = gout[at : at + CH, co * WD : (co + 1) * WD]
        ro, co = ((0, 1), (1, 1), (1, 0))[dx]
        at = (2 * dy + ro) * CH
        g_ref[G_IN + tap * CH : G_IN + (tap + 1) * CH] = gin[at : at + CH, co * WD : (co + 1) * WD]
    if g_ref.shape[0] > G_END:
        g_ref[G_END:] = jnp.zeros((g_ref.shape[0] - G_END, WD), F32)


class Place:
    def __init__(self, dims):
        self.dims = dims
        yl, x, yh, z = dims
        self.chips, self.depth = yh * yl * x, z
        self.la, self.lo = lax.axis_index("lat"), lax.axis_index("lon")
        self.core = lax.rem(self.la, 2)
        self.z = lax.rem(self.lo, z)
        self.chip = ((self.lo // z) * yl + self.la // (2 * x)) * x + lax.rem(self.la // 2, x)

    def in_plane(self, k):
        yl, x, yh, z = self.dims
        chip = lax.rem(self.chip + k, self.chips)
        y = chip // x
        la = (lax.rem(y, yl) * x + lax.rem(chip, x)) * 2 + self.core
        return chip, (la, (y // yl) * z + self.z)

    def sibling(self):
        return (self.la + 1 - 2 * self.core, self.lo)

    def along_z(self, k):
        z = lax.rem(self.z + k, self.depth)
        return z, (self.la, self.lo - self.z + z)


def copy_to(src, dst, ss, rs, dev):
    return pltpu.make_async_remote_copy(
        src_ref=src, dst_ref=dst, send_sem=ss, recv_sem=rs, device_id=dev, device_id_type=MESH
    )


def greet(place, sizes):
    barrier = pltpu.get_barrier_semaphore()
    nla, nlo = sizes
    where = [(lax.rem(place.la + di + nla, nla), lax.rem(place.lo + dj + nlo, nlo)) for di, dj in NB]
    devs = where + [place.sibling()]
    devs += [place.in_plane(k)[1] for k in range(1, place.chips)]
    devs += [place.along_z(k)[1] for k in range(1, place.depth)]
    for dev in devs:
        pl.semaphore_signal(barrier, inc=1, device_id=dev, device_id_type=MESH)
    return where, barrier, len(devs)


def send_edges(where, top_ref, bot_ref, np_ref, nu_ref, nd_ref, n6_ref, ssem, rsem):
    edges = [
        copy_to(top_ref, nd_ref, ssem.at[0], rsem.at[0], where[UP]),
        copy_to(bot_ref, nu_ref, ssem.at[1], rsem.at[1], where[DN]),
    ]
    for k, (di, dj) in enumerate(NB):
        if dj:
            back = NB.index((-di, -dj)) - 2
            edges.append(copy_to(np_ref, n6_ref.at[back], ssem.at[2 + back], rsem.at[2 + back], where[k]))
    for c in edges:
        c.start()
    return edges


def sum_devices(place, g_ref, gs_ref, pair, rel, got, zs, zb, fin, sems):
    n, depth, core = place.chips, place.depth, place.core
    other = 1 - core
    s0, r0, s1, r1, s2, r2, s3, r3, s4, r4 = sems
    sib = place.sibling()
    order = list(range(1, n)) + [0]

    sent = []
    for k in order:
        chip, _ = place.in_plane(k)
        c = copy_to(g_ref.at[other, chip], pair.at[k], s0.at[k], r0.at[k], sib)
        c.start()
        sent.append(c)
    mine = None
    for k in order:
        chip, dev = place.in_plane(k)
        copy_to(g_ref.at[0, 0], pair.at[k], s0.at[k], r0.at[k], sib).wait_recv()
        both = g_ref[core, chip] + pair[k]
        if k:
            rel[k] = both.astype(BF16)
            c = copy_to(rel.at[k], got.at[n - k], s1.at[k], r1.at[n - k], dev)
            c.start()
            sent.append(c)
        else:
            mine = both
    for k in range(1, n):
        copy_to(rel.at[k], got.at[k], s1.at[k], r1.at[k], sib).wait_recv()
        mine = mine + got[k].astype(F32)
    zs[...] = mine.astype(BF16)
    for k in range(1, depth):
        _, dev = place.along_z(k)
        c = copy_to(zs, zb.at[place.z], s2.at[k], r2.at[depth - k], dev)
        c.start()
        sent.append(c)
    zb[place.z] = zs[...]
    for k in range(1, depth):
        z, _ = place.along_z(k)
        copy_to(zs, zb.at[z], s2.at[k], r2.at[k], sib).wait_recv()
    total = zb[0].astype(F32)
    for z in range(1, depth):
        total = total + zb[z].astype(F32)
    fin[...] = total.astype(BF16)
    for k in range(1, n):
        _, dev = place.in_plane(k)
        c = copy_to(fin, gs_ref.at[core, place.chip], s3.at[k], r3.at[n - k], dev)
        c.start()
        sent.append(c)
    c = copy_to(fin, gs_ref.at[core, place.chip], s4.at[0], r4.at[0], sib)
    c.start()
    sent.append(c)
    gs_ref[core, place.chip] = fin[...]
    for k in range(1, n):
        chip, _ = place.in_plane(k)
        copy_to(fin, gs_ref.at[core, chip], s3.at[k], r3.at[k], sib).wait_recv()
        c = copy_to(gs_ref.at[core, chip], gs_ref.at[core, chip], s4.at[k], r4.at[k], sib)
        c.start()
        sent.append(c)
    for k in range(n):
        chip, _ = place.in_plane(k)
        copy_to(fin, gs_ref.at[other, chip], s4.at[k], r4.at[k], sib).wait_recv()
    return sent


def sum_scratch(dims, rows):
    yl, x, yh, z = dims
    n = yl * x * yh
    part = (rows, WD)
    dma = pltpu.SemaphoreType.DMA
    bufs = [pltpu.VMEM((n,) + part, F32)] + [pltpu.VMEM((n,) + part, BF16)] * 2
    bufs += [pltpu.VMEM(part, BF16), pltpu.VMEM((z,) + part, BF16), pltpu.VMEM(part, BF16)]
    return bufs + [dma((m,)) for m in (n, n, n, n, z, z, n, n, n, n)]


def reduce_kernel(sizes, dims, top_ref, bot_ref, np_ref, g_ref, nu_ref, nd_ref, n6_ref, gs_ref, ssem, rsem, *rest):
    place = Place(dims)
    where, barrier, n = greet(place, sizes)
    pl.semaphore_wait(barrier, n)
    edges = send_edges(where, top_ref, bot_ref, np_ref, nu_ref, nd_ref, n6_ref, ssem, rsem)
    sent = sum_devices(place, g_ref, gs_ref, *rest[:6], rest[6:])
    for c in edges:
        c.wait_recv()
    for c in edges + sent:
        c.wait_send()


def finish_kernel(num_ref, inv_ref, nu_ref, nd_ref, n6_ref, g_ref, b_ref, gi_ref, gm_ref, go_ref, scr):
    la, nla = lax.axis_index("lat"), lax.axis_size("lat")
    keep_top = jnp.where(la > 0, 1.0, 0.0).astype(F32)
    keep_bot = jnp.where(la < nla - 1, 1.0, 0.0).astype(F32)
    lane = lanes_of((CH, 128))

    def left_of(k, t):
        v = pltpu.roll(n6_ref[k - 2].astype(F32), (128 - MG * t) % 128, 1) if t else n6_ref[k - 2].astype(F32)
        return jnp.where(lane < MG, v, 0.0)

    def right_of(k, t):
        v = pltpu.roll(n6_ref[k - 2].astype(F32), (64 - MG - MG * t) % 128, 1)
        return jnp.where(lane >= 128 - MG, v, 0.0)

    for r in range(TR):
        v = num_ref[r]
        if r < MG:
            v = v + keep_top * nu_ref[r].astype(F32)
            hl = left_of(LF, r + MG) + keep_top * left_of(UL, r + MG + TR)
            hr = right_of(RT, r + MG) + keep_top * right_of(UR, r + MG + TR)
        else:
            v = v + keep_bot * nd_ref[r - MG].astype(F32)
            hl = left_of(LF, r + MG) + keep_bot * left_of(DL, r - MG)
            hr = right_of(RT, r + MG) + keep_bot * right_of(DR, r - MG)
        v = v + jnp.concatenate([hl, hr], axis=1)
        v = v * inv_ref[r : r + 1, :]
        for half in range(2):
            scr[half, pl.ds(r, CH, stride=TR), :] = v[:, half * 128 : half * 128 + 128]
    for half in range(2):
        b_ref[:, half * 128 : half * 128 + 128] = scr[half]
    for tap in range(9):
        gm_ref[tap] = g_ref[G_MID + tap * WD : G_MID + (tap + 1) * WD].astype(F32)
        go_ref[tap] = g_ref[G_OUT + tap * CH : G_OUT + (tap + 1) * CH].astype(F32)
        gi_ref[tap] = g_ref[G_IN + tap * CH : G_IN + (tap + 1) * CH].astype(F32)


def sds(shape, dtype):
    return jax.ShapeDtypeStruct(shape, dtype)


def shards(sizes, fields, cotangent, kernel_in, kernel_mid, kernel_out, patch_anchors, blend_weights, tile_counts):
    nla, nlo = sizes
    anch = patch_anchors.transpose(0, 1, 3, 2)[0, 0]
    dma = pltpu.SemaphoreType.DMA
    fc, canv, up, dn, en, cn, win, wmid, wout, woutt, wmidt = pl.pallas_call(
        functools.partial(exchange_kernel, sizes),
        name="exchange",
        out_shape=(
            sds((TR, 2 * CH, TC), BF16), sds((2 * TR, EXT), BF16),
            sds((MG, 2 * CH, TC), BF16), sds((MG, 2 * CH, TC), BF16),
            sds((6, 2 * CH, 128), BF16), sds((8, 2 * TR, EXT), BF16),
            sds((2 * WD, 12 * CH), BF16), sds((WD, 9 * WD), BF16), sds((6 * CH, 4 * WD), BF16),
            sds((2 * WD, 12 * CH), BF16), sds((WD, 9 * WD), BF16),
        ),
        in_specs=smem(2) + vmem(6),
        out_specs=vmem(11),
        scratch_shapes=[
            pltpu.VMEM((2 * CH, 128), BF16), pltpu.VMEM((4, CH * TR, 128), F32), dma((16,)), dma((16,)),
        ],
        compiler_params=pltpu.CompilerParams(collective_id=0, has_side_effects=True),
    )(anch, tile_counts, fields, cotangent, blend_weights, kernel_in.transpose(0, 2, 1), kernel_mid, kernel_out)

    dims = (2, 4, 2, 8) if sizes == (16, 16) else (1, nla // 2, 1, nlo)
    parts = dims[0] * dims[1] * dims[2]
    rows = -(-G_END // (16 * parts)) * 8
    grow = 2 * parts * rows
    vm = pltpu.VMEM
    num, top, bot, npk, grads, inv = pl.pallas_call(
        patch_kernel,
        name="patches",
        out_shape=(
            sds((TR, CH, TC), F32), sds((MG, CH, TC), BF16), sds((MG, CH, TC), BF16),
            sds((CH, 128), BF16), sds((grow, WD), F32), sds((TR, TC), F32),
        ),
        in_specs=smem(2) + vmem(12),
        out_specs=vmem(6),
        scratch_shapes=[
            vm((2 * TR, 2 * CH, EXT), BF16), vm((2 * TR, EXT), F32),
            vm((3 * CH, PAD), BF16), vm((3 * CH, PAD), BF16), vm((3 * WD, PAD), BF16), vm((3 * WD, PAD), BF16),
            vm((2 * WD, PAD), BF16), vm((WD, CELLS), F32), vm((WD, CELLS), F32), vm((2 * WD, PAD), BF16),
            vm((2 * TR, CH, EXT), F32), vm((WD, 9 * WD), F32), vm((6 * CH, 2 * WD), F32), vm((6 * CH, 2 * WD), F32),
        ],
    )(anch, tile_counts, fc, up, dn, en, canv, cn, blend_weights, win, wmid, wout, woutt, wmidt)

    nu, nd, n6, gs = pl.pallas_call(
        functools.partial(reduce_kernel, sizes, dims),
        name="reduce",
        out_shape=(
            sds((MG, CH, TC), BF16), sds((MG, CH, TC), BF16), sds((6, CH, 128), BF16),
            sds((2, parts, rows, WD), BF16),
        ),
        in_specs=vmem(4),
        out_specs=vmem(4),
        scratch_shapes=[dma((8,)), dma((8,))] + sum_scratch(dims, rows),
        compiler_params=pltpu.CompilerParams(collective_id=1, has_side_effects=True),
    )(top, bot, npk, grads.reshape(2, parts, rows, WD))

    blended, gi, gm, go = pl.pallas_call(
        finish_kernel,
        name="finish",
        out_shape=(
            sds((CH * TR, TC), F32), sds((9, CH, WD), F32), sds((9, WD, WD), F32), sds((9, CH, WD), F32),
        ),
        in_specs=vmem(6),
        out_specs=vmem(4),
        scratch_shapes=[vm((2, CH * TR, 128), F32)],
    )(num, inv, nu, nd, n6, gs.reshape(grow, WD))
    return blended.reshape(CH, TR, TC), gi.transpose(0, 2, 1), gm, go


def solution(mesh):
    sizes = (mesh.shape["lat"], mesh.shape["lon"])
    return jax.shard_map(
        functools.partial(shards, sizes),
        mesh=mesh,
        in_specs=(
            P(None, "lat", "lon"), P(None, "lat", "lon"), P(), P(), P(),
            P("lat", "lon", None, None), P(None, "lat", "lon"), P("lat", "lon"),
        ),
        out_specs=(P(None, "lat", "lon"), P(), P(), P()),
        check_vma=False,
    )
```
